512 devices in a mesh: row: 32 (over z_lo, y), col: 16 (over x, z_hi, core).
Axes of the slice: x: 4, y: 8, z: 8 (z_hi: 2, z_lo: 4; z = z_hi * 4 + z_lo), core: 2. Of those that a mesh axis runs over, the one named last changes fastest.
Arguments:
- features: bfloat16 [16, 4096, 128], P('col', 'row'), may hold values from -6 to 6
- weight: bfloat16 [128, 256], replicated, may hold values from -0.5 to 0.5
- tile_values: bfloat16 [32, 16, 32, 128, 128], P('row', 'col'), may hold values from -0.125 to 0.125
- tile_rows: int32 [32, 16, 32], P('row', 'col'), may hold values from 0 to 15
- tile_cols: int32 [32, 16, 32], P('row', 'col'), may hold values from 0 to 31
- tile_count: int32 [32, 16], P('row', 'col'), may hold values from 4 to 32, as said below
- cotangent: bfloat16 [32, 2048, 256], P('row', 'col'), may hold values from -6 to 6
Outputs:
- output: bfloat16 [32, 2048, 256], P('row', 'col')
- grad_features: bfloat16 [16, 4096, 128], P('col', 'row')
- weight_grad: float32 [128, 256], replicated
The draws below stay inside these ranges and needn't reach their ends.
Inputs may be any that keep to these rules, and one draw needn't show every extreme that they name: Slots at or beyond a cell's tile_count are ignored; some cell is full in every draw. Tile coordinates within a cell may repeat, and repeated tiles add.
All inputs are finite; a program needn't handle non-finite values.
Results may differ from the reference program's by a relative error of at most 0.022.
Values may be sent and summed in bfloat16 or wider, within the bound.
No kernel may reach another device: no remote copies, remote signals or barrier semaphores. Data moves between devices by JAX's collectives and lax.ppermute only.
A program may use at most 64 MiB of HBM per device.

```python
import jax
import jax.numpy as jnp
from jax import lax

F_IN = 128
F_OUT = 256
TB = 128
ROWS_DEV = 128
TILE_CAP = 32
NODES = 65536
TROWS = 16
TCOLS = 32
N_ROW = 32
N_COL = 16


def draw_tile_count(key, part):
    first_key = jax.random.fold_in(key, 11)
    second_key = jax.random.fold_in(key, 23)
    shifts = jax.random.randint(first_key, (N_ROW, N_COL), 0, 4)
    counts = jnp.right_shift(jnp.full((N_ROW, N_COL), TILE_CAP, jnp.int32), shifts.astype(jnp.int32))
    chosen = jax.random.randint(second_key, (), 0, N_ROW * N_COL)
    positions = jnp.arange(N_ROW * N_COL, dtype=jnp.int32).reshape(N_ROW, N_COL)
    return jnp.where(positions == chosen, TILE_CAP, counts).astype(jnp.int32)


def with_ends(result, rng, least, largest):
    longest = result.shape.index(max(result.shape))
    spots = []
    for shift in (0, 1):
        where = [jax.random.randint(jax.random.fold_in(rng, axis), (), 0, length) for axis, length in enumerate(result.shape)]
        where[longest] = (where[longest] + shift) % result.shape[longest]
        spots.append(tuple(where))
    return result.at[spots[0]].set(least).at[spots[1]].set(largest)


def levels(own_key, dims, cuts, least, top_value):
    level, own = 1.0, jax.random.fold_in(own_key, 6)
    for position, parts in cuts:
        draws = jnp.exp(jax.random.uniform(jax.random.fold_in(own, position), (parts,), jnp.float32, least / len(cuts), top_value / len(cuts)))
        level = level * jnp.repeat(draws, dims[position] // parts).reshape([-1 if axis == position else 1 for axis in range(len(dims))])
    return level


def bell_draw(stream_key, extent, deviation, limit, pieces=(), kind=jnp.bfloat16):
    gain = levels(stream_key, extent, pieces, -0.22, 0.18) if pieces else 1.0
    array = jax.random.normal(stream_key, extent, jnp.float32) * deviation * gain
    return jnp.minimum(jnp.maximum(array, -limit), limit).astype(kind)


def setup_inputs(seed: int = 0) -> dict:
    key_of = jax.random.split(jax.random.key(seed), 8)
    features = bell_draw(key_of[0], (N_COL, NODES // N_COL, F_IN), 1.0, 6.0, ((0, 16), (1, 32)))
    weight = bell_draw(key_of[1], (F_IN, F_OUT), F_IN ** -0.5, 0.5)
    tile_values = bell_draw(key_of[2], (N_ROW, N_COL, TILE_CAP, TB, TB), (TILE_CAP * TB * N_COL // (2 * TROWS)) ** -0.5, 0.125, ((0, 32), (1, 16)))
    tile_rows = with_ends(jax.random.randint(key_of[3], (N_ROW, N_COL, TILE_CAP), 0, TROWS), jax.random.fold_in(key_of[3], 1), 0, TROWS - 1).astype(jnp.int32)
    tile_cols = with_ends(jax.random.randint(key_of[4], (N_ROW, N_COL, TILE_CAP), 0, TCOLS), jax.random.fold_in(key_of[4], 1), 0, TCOLS - 1).astype(jnp.int32)
    tile_count = draw_tile_count(jax.random.fold_in(key_of[7], 71), 0)
    cotangent = bell_draw(key_of[6], (N_ROW, NODES // N_ROW, F_OUT), 1.0, 6.0, ((0, 32), (1, 16)))
    return {"features": features, "weight": weight, "tile_values": tile_values, "tile_rows": tile_rows, "tile_cols": tile_cols, "tile_count": tile_count, "cotangent": cotangent}


def spread_tiles(tile_block, target_ids, source_ids, tile_total, source, out_blocks, transpose):
    source_blocks = source[source_ids].astype(jnp.float32)
    block_float = tile_block.astype(jnp.float32)
    if transpose:
        products = jnp.einsum('tij,tif->tjf', block_float, source_blocks, precision=lax.Precision.HIGHEST)
    else:
        products = jnp.einsum('tij,tjf->tif', block_float, source_blocks, precision=lax.Precision.HIGHEST)
    capacity = tile_block.shape[0]
    live_mask = (jnp.arange(capacity, dtype=jnp.int32) < tile_total).astype(jnp.float32)
    products = products * live_mask[:, None, None]
    return jax.ops.segment_sum(products, target_ids, num_segments=out_blocks)


def reference(features, weight, tile_values, tile_rows, tile_cols, tile_count, cotangent):
    col_source = features.reshape(N_COL, TCOLS, TB, F_IN)

    def forward_row(row_pos):
        def add_cell(running, col_pos):
            term = spread_tiles(tile_values[row_pos, col_pos], tile_rows[row_pos, col_pos], tile_cols[row_pos, col_pos], tile_count[row_pos, col_pos], col_source[col_pos], TROWS, False)
            return running + term, None
        running, unused = lax.scan(add_cell, jnp.zeros((TROWS, TB, F_IN), jnp.float32), jnp.arange(N_COL, dtype=jnp.int32))
        return running

    aggregated = lax.map(forward_row, jnp.arange(N_ROW, dtype=jnp.int32)).astype(jnp.bfloat16)
    agg_flat = aggregated.reshape(N_ROW * ROWS_DEV * N_COL, F_IN)
    pre = jnp.dot(agg_flat, weight, preferred_element_type=jnp.float32)
    sigma = jax.nn.sigmoid(pre)
    output = (pre * sigma).astype(jnp.bfloat16).reshape(N_ROW, ROWS_DEV * N_COL, F_OUT)
    slope = sigma * (1.0 + pre * (1.0 - sigma))
    grad_pre = (cotangent.reshape(-1, F_OUT).astype(jnp.float32) * slope).astype(jnp.bfloat16)
    weight_grad = jnp.dot(agg_flat.T, grad_pre, preferred_element_type=jnp.float32) * (NODES ** -0.5)
    grad_agg = jnp.dot(grad_pre, weight.T, preferred_element_type=jnp.float32).astype(jnp.bfloat16)
    row_source = grad_agg.reshape(N_ROW, TROWS, TB, F_IN)

    def backward_col(col_pos):
        def add_cell(running, row_pos):
            term = spread_tiles(tile_values[row_pos, col_pos], tile_cols[row_pos, col_pos], tile_rows[row_pos, col_pos], tile_count[row_pos, col_pos], row_source[row_pos], TCOLS, True)
            return running + term, None
        running, unused = lax.scan(add_cell, jnp.zeros((TCOLS, TB, F_IN), jnp.float32), jnp.arange(N_ROW, dtype=jnp.int32))
        return running

    grad_features = lax.map(backward_col, jnp.arange(N_COL, dtype=jnp.int32))
    grad_features = grad_features.astype(jnp.bfloat16).reshape(N_COL, ROWS_DEV * N_ROW, F_IN)
    return (output, grad_features, weight_grad)
```

```python
import jax
import jax.numpy as jnp
from jax import lax
from jax.sharding import PartitionSpec as P


def tile_products(tile_block, target_ids, source_ids, tile_total, source, out_blocks, transpose):
    source_blocks = source[source_ids]
    if transpose:
        products = jnp.einsum(
            "tij,tif->tjf", tile_block, source_blocks, preferred_element_type=jnp.float32
        )
    else:
        products = jnp.einsum(
            "tij,tjf->tif", tile_block, source_blocks, preferred_element_type=jnp.float32
        )
    slot_ids = jnp.arange(tile_block.shape[0], dtype=jnp.int32)
    live_mask = slot_ids < tile_total
    one_hot = (
        (target_ids[None, :] == jnp.arange(out_blocks, dtype=jnp.int32)[:, None])
        & live_mask[None, :]
    ).astype(jnp.float32)
    return jnp.einsum("rt,tif->rif", one_hot, products, precision=lax.Precision.HIGH)


def split_f32(x):
    hi = x.astype(jnp.bfloat16)
    lo = (x - hi.astype(jnp.float32)).astype(jnp.bfloat16)
    return hi, lo


def on_device(features, weight, tile_values, tile_rows, tile_cols, tile_count, cotangent):
    rows_dev = features.shape[1]
    width_in = features.shape[2]
    width_out = weight.shape[1]
    tile_size = tile_values.shape[-1]
    n_row = lax.axis_size("row")
    n_col = lax.axis_size("col")
    row_tiles = rows_dev * n_col // tile_size
    col_tiles = rows_dev * n_row // tile_size
    node_total = rows_dev * n_row * n_col
    tile_block = tile_values[0, 0]
    row_ids = tile_rows[0, 0]
    col_ids = tile_cols[0, 0]
    tile_total = tile_count[0, 0]

    own = features[0]
    gathered = lax.all_to_all(
        jnp.broadcast_to(own[None], (n_row,) + own.shape), "row", 0, 0, tiled=False
    )
    col_source = gathered.reshape(col_tiles, tile_size, width_in)
    partial_value = tile_products(tile_block, row_ids, col_ids, tile_total, col_source, row_tiles, False)
    sent = partial_value.reshape(n_col, rows_dev, width_in).astype(jnp.bfloat16)
    got = lax.all_to_all(sent, "col", 0, 0, tiled=False)
    aggregated = got.astype(jnp.float32).sum(0).astype(jnp.bfloat16)

    pre = jnp.dot(aggregated, weight, preferred_element_type=jnp.float32)
    sigma = jax.nn.sigmoid(pre)
    output = (pre * sigma).astype(jnp.bfloat16)[None]
    slope = sigma * (1.0 + pre * (1.0 - sigma))
    grad_pre = (cotangent[0].astype(jnp.float32) * slope).astype(jnp.bfloat16)
    local_grad = lax.dot_general(
        aggregated, grad_pre, (((0,), (0,)), ((), ())), preferred_element_type=jnp.float32
    )
    grad_agg = lax.dot_general(
        grad_pre, weight, (((1,), (1,)), ((), ())), preferred_element_type=jnp.float32
    ).astype(jnp.bfloat16)

    wg_rows = width_in // n_col
    hi, lo = split_f32(local_grad.reshape(n_col, wg_rows, width_out))
    wg_words = jnp.stack([hi, lo], axis=1).reshape(n_col, -1, width_in)
    payload = jnp.concatenate(
        [jnp.broadcast_to(grad_agg[None], (n_col,) + grad_agg.shape), wg_words], axis=1
    )
    got = lax.all_to_all(payload, "col", 0, 0, tiled=False)
    row_source = got[:, :rows_dev].reshape(row_tiles, tile_size, width_in)
    wg_got = got[:, rows_dev:].reshape(n_col, 2, wg_rows * width_out).astype(jnp.float32)
    wg_col = (wg_got[:, 0] + wg_got[:, 1]).sum(0)

    partial_back = tile_products(tile_block, col_ids, row_ids, tile_total, row_source, col_tiles, True)
    piece = wg_col.shape[0] // n_row
    hi, lo = split_f32(wg_col.reshape(n_row, piece))
    wg_words = jnp.concatenate([hi, lo], axis=1).reshape(n_row, 1, 2 * piece)
    payload = jnp.concatenate(
        [partial_back.reshape(n_row, rows_dev, width_in).astype(jnp.bfloat16), wg_words], axis=1
    )
    got = lax.all_to_all(payload, "row", 0, 0, tiled=False)
    grad_features = got[:, :rows_dev].astype(jnp.float32).sum(0).astype(jnp.bfloat16)[None]
    wg_got = got[:, rows_dev].astype(jnp.float32)
    wg_piece = (wg_got[:, :piece] + wg_got[:, piece:]).sum(0)

    n_all = n_row * n_col
    everyone = lax.all_to_all(
        jnp.broadcast_to(wg_piece[None], (n_all, piece)), ("row", "col"), 0, 0, tiled=False
    )
    weight_grad = everyone.reshape(n_row, n_col, piece).transpose(1, 0, 2).reshape(width_in, width_out)
    weight_grad = weight_grad * node_total ** (-0.5)
    return (output, grad_features, weight_grad)


def solution(mesh):
    placed = (
        P("col", "row", None),
        P(),
        P("row", "col", None, None, None),
        P("row", "col", None),
        P("row", "col", None),
        P("row", "col"),
        P("row", "col", None),
    )
    return jax.shard_map(
        on_device,
        mesh=mesh,
        in_specs=placed,
        out_specs=(P("row", "col", None), P("col", "row", None), P()),
        check_vma=False,
    )
```

```python
import functools

import jax
import jax.numpy as jnp
from jax import lax
from jax.experimental import pallas as pl
from jax.experimental.pallas import tpu as pltpu
from jax.sharding import PartitionSpec as P


def spread_kernel(transpose, rows_ref, cols_ref, count_ref, tiles_ref, src_ref, out_ref, acc_ref):
    acc_ref[...] = jnp.zeros_like(acc_ref)
    live = jnp.minimum(count_ref[0], tiles_ref.shape[0])

    def body(t, carry):
        target = rows_ref[t]
        source = cols_ref[t]
        tile = tiles_ref[t]
        if transpose:
            term = lax.dot_general(tile, src_ref[source], (((0,), (0,)), ((), ())),
                                   preferred_element_type=jnp.float32)
        else:
            term = jnp.dot(tile, src_ref[source], preferred_element_type=jnp.float32)
        acc_ref[target] += term
        return carry

    lax.fori_loop(0, live, body, 0)
    out_ref[...] = acc_ref[...].astype(out_ref.dtype)


def spread(tiles, target_ids, source_ids, count, source, out_blocks, transpose, out_dtype):
    slots, tb, _ = tiles.shape
    width = source.shape[-1]
    smem = pl.BlockSpec(memory_space=pltpu.SMEM)
    vmem = pl.BlockSpec(memory_space=pltpu.VMEM)
    return pl.pallas_call(
        functools.partial(spread_kernel, transpose),
        out_shape=jax.ShapeDtypeStruct((out_blocks, tb, width), out_dtype),
        in_specs=[smem, smem, smem, vmem, vmem],
        out_specs=vmem,
        scratch_shapes=[pltpu.VMEM((out_blocks, tb, width), jnp.float32)],
        cost_estimate=pl.CostEstimate(
            flops=2 * slots * tb * tb * width, transcendentals=0,
            bytes_accessed=tiles.size * 2 + source.size * 2 + out_blocks * tb * width * 2),
    )(target_ids, source_ids, count.reshape(1), tiles, source)


def split_f32(x):
    hi = x.astype(jnp.bfloat16)
    lo = (x - hi.astype(jnp.float32)).astype(jnp.bfloat16)
    return hi, lo


def on_device(features, weight, tile_values, tile_rows, tile_cols, tile_count, cotangent):
    rows_dev = features.shape[1]
    width_in = features.shape[2]
    width_out = weight.shape[1]
    tile_size = tile_values.shape[-1]
    n_row = lax.axis_size("row")
    n_col = lax.axis_size("col")
    row_tiles = rows_dev * n_col // tile_size
    col_tiles = rows_dev * n_row // tile_size
    node_total = rows_dev * n_row * n_col
    tile_block = tile_values[0, 0]
    row_ids = tile_rows[0, 0]
    col_ids = tile_cols[0, 0]
    tile_total = tile_count[0, 0]

    own = features[0]
    gathered = lax.all_to_all(
        jnp.broadcast_to(own[None], (n_row,) + own.shape), "row", 0, 0, tiled=False
    )
    col_source = gathered.reshape(col_tiles, tile_size, width_in)
    partial_value = spread(tile_block, row_ids, col_ids, tile_total, col_source, row_tiles, False, jnp.bfloat16)
    sent = partial_value.reshape(n_col, rows_dev, width_in)
    got = lax.all_to_all(sent, "col", 0, 0, tiled=False)
    aggregated = got.astype(jnp.float32).sum(0).astype(jnp.bfloat16)

    pre = jnp.dot(aggregated, weight, preferred_element_type=jnp.float32)
    sigma = jax.nn.sigmoid(pre)
    output = (pre * sigma).astype(jnp.bfloat16)[None]
    slope = sigma * (1.0 + pre * (1.0 - sigma))
    grad_pre = (cotangent[0].astype(jnp.float32) * slope).astype(jnp.bfloat16)
    local_grad = lax.dot_general(
        aggregated, grad_pre, (((0,), (0,)), ((), ())), preferred_element_type=jnp.float32
    )
    grad_agg = lax.dot_general(
        grad_pre, weight, (((1,), (1,)), ((), ())), preferred_element_type=jnp.float32
    ).astype(jnp.bfloat16)

    wg_rows = width_in // n_col
    hi, lo = split_f32(local_grad.reshape(n_col, wg_rows, width_out))
    wg_words = jnp.stack([hi, lo], axis=1).reshape(n_col, -1, width_in)
    payload = jnp.concatenate(
        [jnp.broadcast_to(grad_agg[None], (n_col,) + grad_agg.shape), wg_words], axis=1
    )
    got = lax.all_to_all(payload, "col", 0, 0, tiled=False)
    row_source = got[:, :rows_dev].reshape(row_tiles, tile_size, width_in)
    wg_got = got[:, rows_dev:].reshape(n_col, 2, wg_rows * width_out).astype(jnp.float32)
    wg_col = (wg_got[:, 0] + wg_got[:, 1]).sum(0)

    partial_back = spread(tile_block, col_ids, row_ids, tile_total, row_source, col_tiles, True, jnp.bfloat16)
    piece = wg_col.shape[0] // n_row
    hi, lo = split_f32(wg_col.reshape(n_row, piece))
    wg_words = jnp.concatenate([hi, lo], axis=1).reshape(n_row, 1, 2 * piece)
    payload = jnp.concatenate(
        [partial_back.reshape(n_row, rows_dev, width_in), wg_words], axis=1
    )
    got = lax.all_to_all(payload, "row", 0, 0, tiled=False)
    grad_features = got[:, :rows_dev].astype(jnp.float32).sum(0).astype(jnp.bfloat16)[None]
    wg_got = got[:, rows_dev].astype(jnp.float32)
    wg_piece = (wg_got[:, :piece] + wg_got[:, piece:]).sum(0)

    n_all = n_row * n_col
    everyone = lax.all_to_all(
        jnp.broadcast_to(wg_piece[None], (n_all, piece)), ("row", "col"), 0, 0, tiled=False
    )
    weight_grad = everyone.reshape(n_row, n_col, piece).transpose(1, 0, 2).reshape(width_in, width_out)
    weight_grad = weight_grad * node_total ** (-0.5)
    return (output, grad_features, weight_grad)


def solution(mesh):
    placed = (
        P("col", "row", None),
        P(),
        P("row", "col", None, None, None),
        P("row", "col", None),
        P("row", "col", None),
        P("row", "col"),
        P("row", "col", None),
    )
    return jax.shard_map(
        on_device,
        mesh=mesh,
        in_specs=placed,
        out_specs=(P("row", "col", None), P("col", "row", None), P()),
        check_vma=False,
    )
```

```python
import functools

import jax
import jax.numpy as jnp
from jax import lax
from jax.experimental import pallas as pl
from jax.experimental.pallas import tpu as pltpu
from jax.sharding import PartitionSpec as P


def spread_kernel(transpose, rows_ref, cols_ref, count_ref, tiles_ref, src_ref, *rest):
    if len(rest) == 3:
        extra_ref, out_ref, acc_ref = rest
    else:
        extra_ref = None
        out_ref, acc_ref = rest
    tb = tiles_ref.shape[1]
    acc_ref[...] = jnp.zeros_like(acc_ref)
    live = count_ref[0]
    for t in range(tiles_ref.shape[0]):
        tile = tiles_ref[t]
        src = src_ref[cols_ref[t]]
        if transpose:
            term = lax.dot_general(tile, src, (((0,), (0,)), ((), ())),
                                   preferred_element_type=jnp.float32)
        else:
            term = jnp.dot(tile, src, preferred_element_type=jnp.float32)
        acc_ref[rows_ref[t]] += jnp.where(t < live, term, 0.0)
    if extra_ref is None:
        out_ref[...] = acc_ref[...].astype(out_ref.dtype)
    else:
        out_ref[:, :tb, :] = acc_ref[...].astype(out_ref.dtype)
        out_ref[:, tb:, :] = extra_ref[...]


def spread(tiles, target_ids, source_ids, count, source, out_blocks, transpose, out_dtype, extra=None):
    slots, tb, _ = tiles.shape
    width = source.shape[-1]
    smem = pl.BlockSpec(memory_space=pltpu.SMEM)
    vmem = pl.BlockSpec(memory_space=pltpu.VMEM)
    args = [target_ids, source_ids, count.reshape(1), tiles, source]
    out_rows = tb
    if extra is not None:
        args.append(extra)
        out_rows += extra.shape[1]
    return pl.pallas_call(
        functools.partial(spread_kernel, transpose),
        out_shape=jax.ShapeDtypeStruct((out_blocks, out_rows, width), out_dtype),
        in_specs=[smem, smem, smem] + [vmem] * (len(args) - 3),
        out_specs=vmem,
        scratch_shapes=[pltpu.VMEM((out_blocks, tb, width), jnp.float32)],
        cost_estimate=pl.CostEstimate(
            flops=2 * slots * tb * tb * width, transcendentals=0,
            bytes_accessed=tiles.size * 2 + source.size * 2 + out_blocks * out_rows * width * 2),
    )(*args)


def split_f32(x):
    hi = x.astype(jnp.bfloat16)
    lo = (x - hi.astype(jnp.float32)).astype(jnp.bfloat16)
    return hi, lo


def on_device(features, weight, tile_values, tile_rows, tile_cols, tile_count, cotangent):
    rows_dev = features.shape[1]
    width_in = features.shape[2]
    width_out = weight.shape[1]
    tile_size = tile_values.shape[-1]
    n_row = lax.axis_size("row")
    n_col = lax.axis_size("col")
    row_tiles = rows_dev * n_col // tile_size
    col_tiles = rows_dev * n_row // tile_size
    node_total = rows_dev * n_row * n_col
    tile_block = tile_values[0, 0]
    row_ids = tile_rows[0, 0]
    col_ids = tile_cols[0, 0]
    tile_total = tile_count[0, 0]

    own = features[0]
    gathered = lax.all_to_all(
        jnp.broadcast_to(own[None], (n_row,) + own.shape), "row", 0, 0, tiled=False
    )
    col_source = gathered.reshape(col_tiles, tile_size, width_in)
    partial_value = spread(tile_block, row_ids, col_ids, tile_total, col_source, row_tiles, False, jnp.bfloat16)
    sent = partial_value.reshape(n_col, rows_dev, width_in)
    got = lax.all_to_all(sent, "col", 0, 0, tiled=False)
    aggregated = got.astype(jnp.float32).sum(0).astype(jnp.bfloat16)

    pre = jnp.dot(aggregated, weight, preferred_element_type=jnp.float32)
    sigma = jax.nn.sigmoid(pre)
    output = (pre * sigma).astype(jnp.bfloat16)[None]
    slope = sigma * (1.0 + pre * (1.0 - sigma))
    grad_pre = (cotangent[0].astype(jnp.float32) * slope).astype(jnp.bfloat16)
    local_grad = lax.dot_general(
        aggregated, grad_pre, (((0,), (0,)), ((), ())), preferred_element_type=jnp.float32
    )
    grad_agg = lax.dot_general(
        grad_pre, weight, (((1,), (1,)), ((), ())), preferred_element_type=jnp.float32
    ).astype(jnp.bfloat16)

    wg_rows = width_in // n_col
    hi, lo = split_f32(local_grad.reshape(n_col, wg_rows, width_out))
    wg_words = jnp.stack([hi, lo], axis=1).reshape(n_col, -1, width_in)
    payload = jnp.concatenate(
        [jnp.broadcast_to(grad_agg[None], (n_col,) + grad_agg.shape), wg_words], axis=1
    )
    got = lax.all_to_all(payload, "col", 0, 0, tiled=False)
    row_source = got[:, :rows_dev].reshape(row_tiles, tile_size, width_in)
    wg_got = got[:, rows_dev:].reshape(n_col, 2, wg_rows * width_out).astype(jnp.float32)
    wg_col = (wg_got[:, 0] + wg_got[:, 1]).sum(0)

    piece = wg_col.shape[0] // n_row
    hi, lo = split_f32(wg_col.reshape(n_row, piece))
    wg_words = jnp.concatenate([hi, lo], axis=1).reshape(n_row, -1, width_in)
    pad_rows = 16 - wg_words.shape[1] % 16
    wg_words = jnp.pad(wg_words, ((0, 0), (0, pad_rows), (0, 0)))
    payload = spread(
        tile_block, col_ids, row_ids, tile_total, row_source, col_tiles, True, jnp.bfloat16, wg_words
    )
    got = lax.all_to_all(payload, "row", 0, 0, tiled=False)
    grad_features = got[:, :rows_dev].astype(jnp.float32).sum(0).astype(jnp.bfloat16)[None]
    wg_got = got[:, rows_dev:].reshape(n_row, -1)[:, : 2 * piece].astype(jnp.float32)
    wg_piece = (wg_got[:, :piece] + wg_got[:, piece:]).sum(0)

    n_all = n_row * n_col
    everyone = lax.all_to_all(
        jnp.broadcast_to(wg_piece[None], (n_all, piece)), ("row", "col"), 0, 0, tiled=False
    )
    weight_grad = everyone.reshape(n_row, n_col, piece).transpose(1, 0, 2).reshape(width_in, width_out)
    weight_grad = weight_grad * node_total ** (-0.5)
    return (output, grad_features, weight_grad)


def solution(mesh):
    placed = (
        P("col", "row", None),
        P(),
        P("row", "col", None, None, None),
        P("row", "col", None),
        P("row", "col", None),
        P("row", "col"),
        P("row", "col", None),
    )
    return jax.shard_map(
        on_device,
        mesh=mesh,
        in_specs=placed,
        out_specs=(P("row", "col", None), P("col", "row", None), P()),
        check_vma=False,
    )
```

```python
import functools

import jax
import jax.numpy as jnp
from jax import lax
from jax.experimental import pallas as pl
from jax.experimental.pallas import tpu as pltpu
from jax.sharding import PartitionSpec as P


def spread_kernel(transpose, rows_ref, cols_ref, count_ref, tiles_ref, src_ref, *rest):
    if len(rest) == 3:
        extra_ref, out_ref, acc_ref = rest
    else:
        extra_ref = None
        out_ref, acc_ref = rest
    tb = tiles_ref.shape[1]
    acc_ref[...] = jnp.zeros_like(acc_ref)
    live = count_ref[0]
    for t in range(tiles_ref.shape[0]):
        tile = tiles_ref[t]
        src = src_ref[cols_ref[t], :tb, :]
        if transpose:
            term = lax.dot_general(tile, src, (((0,), (0,)), ((), ())),
                                   preferred_element_type=jnp.float32)
        else:
            term = jnp.dot(tile, src, preferred_element_type=jnp.float32)
        acc_ref[rows_ref[t]] += jnp.where(t < live, term, 0.0)
    if extra_ref is None:
        out_ref[...] = acc_ref[...].astype(out_ref.dtype)
    else:
        out_ref[:, :tb, :] = acc_ref[...].astype(out_ref.dtype)
        words = extra_ref.shape[1]
        out_ref[:, tb:tb + words, :] = extra_ref[...]
        out_ref[:, tb + words:, :] = jnp.zeros(
            (out_ref.shape[0], out_ref.shape[1] - tb - words, out_ref.shape[2]), out_ref.dtype)


def spread(tiles, target_ids, source_ids, count, source, out_blocks, transpose, out_dtype, extra=None):
    slots, tb, _ = tiles.shape
    width = source.shape[-1]
    smem = pl.BlockSpec(memory_space=pltpu.SMEM)
    vmem = pl.BlockSpec(memory_space=pltpu.VMEM)
    args = [target_ids, source_ids, count.reshape(1), tiles, source]
    out_rows = tb
    if extra is not None:
        args.append(extra)
        out_rows += -(-extra.shape[1] // 16) * 16
    return pl.pallas_call(
        functools.partial(spread_kernel, transpose),
        out_shape=jax.ShapeDtypeStruct((out_blocks, out_rows, width), out_dtype),
        in_specs=[smem, smem, smem] + [vmem] * (len(args) - 3),
        out_specs=vmem,
        scratch_shapes=[pltpu.VMEM((out_blocks, tb, width), jnp.float32)],
        cost_estimate=pl.CostEstimate(
            flops=2 * slots * tb * tb * width, transcendentals=0,
            bytes_accessed=tiles.size * 2 + source.size * 2 + out_blocks * out_rows * width * 2),
    )(*args)


def split_f32(x):
    hi = x.astype(jnp.bfloat16)
    lo = (x - hi.astype(jnp.float32)).astype(jnp.bfloat16)
    return hi, lo


def on_device(features, weight, tile_values, tile_rows, tile_cols, tile_count, cotangent):
    rows_dev = features.shape[1]
    width_in = features.shape[2]
    width_out = weight.shape[1]
    tile_size = tile_values.shape[-1]
    n_row = lax.axis_size("row")
    n_col = lax.axis_size("col")
    row_tiles = rows_dev * n_col // tile_size
    col_tiles = rows_dev * n_row // tile_size
    node_total = rows_dev * n_row * n_col
    tile_block = tile_values[0, 0]
    row_ids = tile_rows[0, 0]
    col_ids = tile_cols[0, 0]
    tile_total = tile_count[0, 0]

    own = features[0]
    gathered = lax.all_to_all(
        jnp.broadcast_to(own[None], (n_row,) + own.shape), "row", 0, 0, tiled=False
    )
    col_source = gathered.reshape(col_tiles, tile_size, width_in)
    partial_value = spread(tile_block, row_ids, col_ids, tile_total, col_source, row_tiles, False, jnp.bfloat16)
    sent = partial_value.reshape(n_col, rows_dev, width_in)
    got = lax.all_to_all(sent, "col", 0, 0, tiled=False)
    aggregated = got.astype(jnp.float32).sum(0).astype(jnp.bfloat16)

    pre = jnp.dot(aggregated, weight, preferred_element_type=jnp.float32)
    sigma = jax.nn.sigmoid(pre)
    output = (pre * sigma).astype(jnp.bfloat16)[None]
    slope = sigma * (1.0 + pre * (1.0 - sigma))
    grad_pre = (cotangent[0].astype(jnp.float32) * slope).astype(jnp.bfloat16)
    local_grad = lax.dot_general(
        aggregated, grad_pre, (((0,), (0,)), ((), ())), preferred_element_type=jnp.float32
    )
    grad_agg = lax.dot_general(
        grad_pre, weight, (((1,), (1,)), ((), ())), preferred_element_type=jnp.float32
    ).astype(jnp.bfloat16)

    wg_rows = width_in // n_col
    hi, lo = split_f32(local_grad.reshape(n_col, wg_rows, width_out))
    wg_words = jnp.stack([hi, lo], axis=1).reshape(n_col, -1, width_in)
    payload = jnp.concatenate(
        [jnp.broadcast_to(grad_agg[None], (n_col,) + grad_agg.shape), wg_words], axis=1
    )
    got = lax.all_to_all(payload, "col", 0, 0, tiled=False)
    row_source = got
    wg_got = got[:, rows_dev:].reshape(n_col, 2, wg_rows * width_out).astype(jnp.float32)
    wg_col = (wg_got[:, 0] + wg_got[:, 1]).sum(0)

    piece = wg_col.shape[0] // n_row
    hi, lo = split_f32(wg_col.reshape(n_row, piece))
    wg_words = jnp.concatenate([hi, lo], axis=1).reshape(n_row, -1, width_in)
    payload = spread(
        tile_block, col_ids, row_ids, tile_total, row_source, col_tiles, True, jnp.bfloat16, wg_words
    )
    got = lax.all_to_all(payload, "row", 0, 0, tiled=False)
    grad_features = got[:, :rows_dev].astype(jnp.float32).sum(0).astype(jnp.bfloat16)[None]
    wg_got = got[:, rows_dev:].reshape(n_row, -1)[:, : 2 * piece].astype(jnp.float32)
    wg_piece = (wg_got[:, :piece] + wg_got[:, piece:]).sum(0)

    n_all = n_row * n_col
    everyone = lax.all_to_all(
        jnp.broadcast_to(wg_piece[None], (n_all, piece)), ("row", "col"), 0, 0, tiled=False
    )
    weight_grad = everyone.reshape(n_row, n_col, piece).transpose(1, 0, 2).reshape(width_in, width_out)
    weight_grad = weight_grad * node_total ** (-0.5)
    return (output, grad_features, weight_grad)


def solution(mesh):
    placed = (
        P("col", "row", None),
        P(),
        P("row", "col", None, None, None),
        P("row", "col", None),
        P("row", "col", None),
        P("row", "col"),
        P("row", "col", None),
    )
    return jax.shard_map(
        on_device,
        mesh=mesh,
        in_specs=placed,
        out_specs=(P("row", "col", None), P("col", "row", None), P()),
        check_vma=False,
    )
```

```python
import functools

import jax
import jax.numpy as jnp
from jax import lax
from jax.experimental import pallas as pl
from jax.experimental.pallas import tpu as pltpu
from jax.sharding import PartitionSpec as P


def spread_kernel(transpose, rows_ref, cols_ref, count_ref, tiles_ref, src_ref, *rest):
    if len(rest) == 3:
        extra_ref, out_ref, acc_ref = rest
    else:
        extra_ref = None
        out_ref, acc_ref = rest
    tb = tiles_ref.shape[1]
    acc_ref[...] = jnp.zeros_like(acc_ref)
    live = count_ref[0]
    for t in range(tiles_ref.shape[0]):
        tile = tiles_ref[t]
        src = src_ref[cols_ref[t], :tb, :]
        if transpose:
            term = lax.dot_general(tile, src, (((0,), (0,)), ((), ())),
                                   preferred_element_type=jnp.float32)
        else:
            term = jnp.dot(tile, src, preferred_element_type=jnp.float32)
        acc_ref[rows_ref[t]] += jnp.where(t < live, term, 0.0)
    if extra_ref is None:
        out_ref[...] = acc_ref[...].astype(out_ref.dtype)
    else:
        out_ref[:, :tb, :] = acc_ref[...].astype(out_ref.dtype)
        words = extra_ref.shape[1]
        out_ref[:, tb:tb + words, :] = extra_ref[...]
        out_ref[:, tb + words:, :] = jnp.zeros(
            (out_ref.shape[0], out_ref.shape[1] - tb - words, out_ref.shape[2]), out_ref.dtype)


def spread(tiles, target_ids, source_ids, count, source, out_blocks, transpose, out_dtype, extra=None):
    slots, tb, _ = tiles.shape
    width = source.shape[-1]
    smem = pl.BlockSpec(memory_space=pltpu.SMEM)
    vmem = pl.BlockSpec(memory_space=pltpu.VMEM)
    args = [target_ids, source_ids, count.reshape(1), tiles, source]
    out_rows = tb
    if extra is not None:
        args.append(extra)
        out_rows += -(-extra.shape[1] // 16) * 16
    return pl.pallas_call(
        functools.partial(spread_kernel, transpose),
        out_shape=jax.ShapeDtypeStruct((out_blocks, out_rows, width), out_dtype),
        in_specs=[smem, smem, smem] + [vmem] * (len(args) - 3),
        out_specs=vmem,
        scratch_shapes=[pltpu.VMEM((out_blocks, tb, width), jnp.float32)],
        cost_estimate=pl.CostEstimate(
            flops=2 * slots * tb * tb * width, transcendentals=0,
            bytes_accessed=tiles.size * 2 + source.size * 2 + out_blocks * out_rows * width * 2),
    )(*args)


def split_f32(x):
    hi = x.astype(jnp.bfloat16)
    lo = (x - hi.astype(jnp.float32)).astype(jnp.bfloat16)
    return hi, lo


def replicate_kernel(x_ref, out_ref):
    out_ref[...] = jnp.broadcast_to(x_ref[...], out_ref.shape)


def replicate(x, copies):
    vmem = pl.BlockSpec(memory_space=pltpu.VMEM)
    return pl.pallas_call(
        replicate_kernel,
        out_shape=jax.ShapeDtypeStruct((copies,) + x.shape[1:], x.dtype),
        in_specs=[vmem],
        out_specs=vmem,
        cost_estimate=pl.CostEstimate(
            flops=0, transcendentals=0, bytes_accessed=(copies + 1) * x.size * x.dtype.itemsize),
    )(x)


def on_device(features, weight, tile_values, tile_rows, tile_cols, tile_count, cotangent):
    rows_dev = features.shape[1]
    width_in = features.shape[2]
    width_out = weight.shape[1]
    tile_size = tile_values.shape[-1]
    n_row = lax.axis_size("row")
    n_col = lax.axis_size("col")
    row_tiles = rows_dev * n_col // tile_size
    col_tiles = rows_dev * n_row // tile_size
    node_total = rows_dev * n_row * n_col
    tile_block = tile_values[0, 0]
    row_ids = tile_rows[0, 0]
    col_ids = tile_cols[0, 0]
    tile_total = tile_count[0, 0]

    gathered = lax.all_to_all(replicate(features, n_row), "row", 0, 0, tiled=False)
    col_source = gathered.reshape(col_tiles, tile_size, width_in)
    partial_value = spread(tile_block, row_ids, col_ids, tile_total, col_source, row_tiles, False, jnp.bfloat16)
    sent = partial_value.reshape(n_col, rows_dev, width_in)
    got = lax.all_to_all(sent, "col", 0, 0, tiled=False)
    aggregated = got.astype(jnp.float32).sum(0).astype(jnp.bfloat16)

    pre = jnp.dot(aggregated, weight, preferred_element_type=jnp.float32)
    sigma = jax.nn.sigmoid(pre)
    output = (pre * sigma).astype(jnp.bfloat16)[None]
    slope = sigma * (1.0 + pre * (1.0 - sigma))
    grad_pre = (cotangent[0].astype(jnp.float32) * slope).astype(jnp.bfloat16)
    local_grad = lax.dot_general(
        aggregated, grad_pre, (((0,), (0,)), ((), ())), preferred_element_type=jnp.float32
    )
    grad_agg = lax.dot_general(
        grad_pre, weight, (((1,), (1,)), ((), ())), preferred_element_type=jnp.float32
    ).astype(jnp.bfloat16)

    wg_rows = width_in // n_col
    hi, lo = split_f32(local_grad.reshape(n_col, wg_rows, width_out))
    wg_words = jnp.stack([hi, lo], axis=1).reshape(n_col, -1, width_in)
    payload = jnp.concatenate(
        [jnp.broadcast_to(grad_agg[None], (n_col,) + grad_agg.shape), wg_words], axis=1
    )
    got = lax.all_to_all(payload, "col", 0, 0, tiled=False)
    row_source = got
    wg_got = got[:, rows_dev:].reshape(n_col, 2, wg_rows * width_out).astype(jnp.float32)
    wg_col = (wg_got[:, 0] + wg_got[:, 1]).sum(0)

    piece = wg_col.shape[0] // n_row
    hi, lo = split_f32(wg_col.reshape(n_row, piece))
    wg_words = jnp.concatenate([hi, lo], axis=1).reshape(n_row, -1, width_in)
    payload = spread(
        tile_block, col_ids, row_ids, tile_total, row_source, col_tiles, True, jnp.bfloat16, wg_words
    )
    got = lax.all_to_all(payload, "row", 0, 0, tiled=False)
    grad_features = got[:, :rows_dev].astype(jnp.float32).sum(0).astype(jnp.bfloat16)[None]
    wg_got = got[:, rows_dev:].reshape(n_row, -1)[:, : 2 * piece].astype(jnp.float32)
    wg_piece = (wg_got[:, :piece] + wg_got[:, piece:]).sum(0)

    n_all = n_row * n_col
    wg_piece = wg_piece * node_total ** (-0.5)
    everyone = lax.all_to_all(
        jnp.broadcast_to(wg_piece[None], (n_all, piece)), ("col", "row"), 0, 0, tiled=True
    )
    weight_grad = everyone.reshape(width_in, width_out)
    return (output, grad_features, weight_grad)


def solution(mesh):
    placed = (
        P("col", "row", None),
        P(),
        P("row", "col", None, None, None),
        P("row", "col", None),
        P("row", "col", None),
        P("row", "col"),
        P("row", "col", None),
    )
    return jax.shard_map(
        on_device,
        mesh=mesh,
        in_specs=placed,
        out_specs=(P("row", "col", None), P("col", "row", None), P()),
        check_vma=False,
    )
```

```python
import functools

import jax
import jax.numpy as jnp
from jax import lax
from jax.experimental import pallas as pl
from jax.experimental.pallas import tpu as pltpu
from jax.sharding import PartitionSpec as P


def spread_kernel(transpose, rows_ref, cols_ref, count_ref, tiles_ref, src_ref, *rest):
    if len(rest) == 3:
        extra_ref, out_ref, acc_ref = rest
    else:
        extra_ref = None
        out_ref, acc_ref = rest
    tb = tiles_ref.shape[1]
    acc_ref[...] = jnp.zeros_like(acc_ref)
    live = count_ref[0]
    for t in range(tiles_ref.shape[0]):
        tile = tiles_ref[t]
        src = src_ref[cols_ref[t], :tb, :]
        if transpose:
            term = lax.dot_general(tile, src, (((0,), (0,)), ((), ())),
                                   preferred_element_type=jnp.float32)
        else:
            term = jnp.dot(tile, src, preferred_element_type=jnp.float32)
        acc_ref[rows_ref[t]] += jnp.where(t < live, term, 0.0)
    if extra_ref is None:
        out_ref[...] = acc_ref[...].astype(out_ref.dtype)
    else:
        out_ref[:, :tb, :] = acc_ref[...].astype(out_ref.dtype)
        out_ref[:, tb:, :] = jnp.broadcast_to(extra_ref[...][None], (out_ref.shape[0],) + extra_ref.shape)


def spread(tiles, target_ids, source_ids, count, source, out_blocks, transpose, out_dtype, extra=None):
    slots, tb, _ = tiles.shape
    width = source.shape[-1]
    smem = pl.BlockSpec(memory_space=pltpu.SMEM)
    vmem = pl.BlockSpec(memory_space=pltpu.VMEM)
    args = [target_ids, source_ids, count.reshape(1), tiles, source]
    out_rows = tb
    if extra is not None:
        args.append(extra)
        out_rows += extra.shape[0]
    return pl.pallas_call(
        functools.partial(spread_kernel, transpose),
        out_shape=jax.ShapeDtypeStruct((out_blocks, out_rows, width), out_dtype),
        in_specs=[smem, smem, smem] + [vmem] * (len(args) - 3),
        out_specs=vmem,
        scratch_shapes=[pltpu.VMEM((out_blocks, tb, width), jnp.float32)],
        cost_estimate=pl.CostEstimate(
            flops=2 * slots * tb * tb * width, transcendentals=0,
            bytes_accessed=tiles.size * 2 + source.size * 2 + out_blocks * out_rows * width * 2),
    )(*args)


def split_f32(x):
    hi = x.astype(jnp.bfloat16)
    lo = (x - hi.astype(jnp.float32)).astype(jnp.bfloat16)
    return hi, lo


def on_device(features, weight, tile_values, tile_rows, tile_cols, tile_count, cotangent):
    rows_dev = features.shape[1]
    width_in = features.shape[2]
    width_out = weight.shape[1]
    tile_size = tile_values.shape[-1]
    n_row = lax.axis_size("row")
    n_col = lax.axis_size("col")
    row_tiles = rows_dev * n_col // tile_size
    col_tiles = rows_dev * n_row // tile_size
    node_total = rows_dev * n_row * n_col
    tile_block = tile_values[0, 0]
    row_ids = tile_rows[0, 0]
    col_ids = tile_cols[0, 0]
    tile_total = tile_count[0, 0]

    own = features[0]
    gathered = lax.all_to_all(
        jnp.broadcast_to(own[None], (n_row,) + own.shape), "row", 0, 0, tiled=False
    )
    col_source = gathered.reshape(col_tiles, tile_size, width_in)
    partial_value = spread(tile_block, row_ids, col_ids, tile_total, col_source, row_tiles, False, jnp.bfloat16)
    sent = partial_value.reshape(n_col, rows_dev, width_in)
    got = lax.all_to_all(sent, "col", 0, 0, tiled=False)
    aggregated = got.astype(jnp.float32).sum(0).astype(jnp.bfloat16)

    pre = jnp.dot(aggregated, weight, preferred_element_type=jnp.float32)
    sigma = jax.nn.sigmoid(pre)
    output = (pre * sigma).astype(jnp.bfloat16)[None]
    slope = sigma * (1.0 + pre * (1.0 - sigma))
    grad_pre = (cotangent[0].astype(jnp.float32) * slope).astype(jnp.bfloat16)
    local_grad = lax.dot_general(
        aggregated, grad_pre, (((0,), (0,)), ((), ())), preferred_element_type=jnp.float32
    )
    grad_agg = lax.dot_general(
        grad_pre, weight, (((1,), (1,)), ((), ())), preferred_element_type=jnp.float32
    ).astype(jnp.bfloat16)

    wg_rows = width_in // n_col
    hi, lo = split_f32(local_grad.reshape(n_col, wg_rows, width_out))
    wg_words = jnp.stack([hi, lo], axis=1).reshape(n_col, -1, width_in)
    payload = jnp.concatenate(
        [jnp.broadcast_to(grad_agg[None], (n_col,) + grad_agg.shape), wg_words], axis=1
    )
    got = lax.all_to_all(payload, "col", 0, 0, tiled=False)
    row_source = got
    wg_got = got[:, rows_dev:].reshape(n_col, 2, wg_rows * width_out).astype(jnp.float32)
    wg_col = (wg_got[:, 0] + wg_got[:, 1]).sum(0)

    hi, lo = split_f32(wg_col)
    wg_words = jnp.stack([hi, lo]).reshape(-1, width_in)
    payload = spread(
        tile_block, col_ids, row_ids, tile_total, row_source, col_tiles, True, jnp.bfloat16, wg_words
    )
    got = lax.all_to_all(payload, "row", 0, 0, tiled=False)
    grad_features = got[:, :rows_dev].astype(jnp.float32).sum(0).astype(jnp.bfloat16)[None]
    wg_got = got[:, rows_dev:].reshape(n_row, 2, -1).astype(jnp.float32)
    wg_part = (wg_got[:, 0] + wg_got[:, 1]).sum(0) * node_total ** (-0.5)

    everyone = lax.all_to_all(
        jnp.broadcast_to(wg_part[None], (n_col,) + wg_part.shape), "col", 0, 0, tiled=False
    )
    weight_grad = everyone.reshape(width_in, width_out)
    return (output, grad_features, weight_grad)


def solution(mesh):
    placed = (
        P("col", "row", None),
        P(),
        P("row", "col", None, None, None),
        P("row", "col", None),
        P("row", "col", None),
        P("row", "col"),
        P("row", "col", None),
    )
    return jax.shard_map(
        on_device,
        mesh=mesh,
        in_specs=placed,
        out_specs=(P("row", "col", None), P("col", "row", None), P()),
        check_vma=False,
    )
```

```python
import functools

import jax
import jax.numpy as jnp
from jax import lax
from jax.experimental import pallas as pl
from jax.experimental.pallas import tpu as pltpu
from jax.sharding import PartitionSpec as P


def spread_kernel(transpose, rows_ref, cols_ref, count_ref, tiles_ref, src_ref, *rest):
    if len(rest) == 3:
        extra_ref, out_ref, acc_ref = rest
    else:
        extra_ref = None
        out_ref, acc_ref = rest
    tb = tiles_ref.shape[1]
    acc_ref[...] = jnp.zeros_like(acc_ref)
    live = count_ref[0]
    for t in range(tiles_ref.shape[0]):
        tile = tiles_ref[t]
        src = src_ref[cols_ref[t], :tb, :]
        if transpose:
            term = lax.dot_general(tile, src, (((0,), (0,)), ((), ())),
                                   preferred_element_type=jnp.float32)
        else:
            term = jnp.dot(tile, src, preferred_element_type=jnp.float32)
        acc_ref[rows_ref[t]] += jnp.where(t < live, term, 0.0)
    if extra_ref is None:
        out_ref[...] = acc_ref[...].astype(out_ref.dtype)
    else:
        out_ref[:, :tb, :] = acc_ref[...].astype(out_ref.dtype)
        out_ref[:, tb:, :] = jnp.broadcast_to(extra_ref[...][None], (out_ref.shape[0],) + extra_ref.shape)


def spread(tiles, target_ids, source_ids, count, source, out_blocks, transpose, out_dtype, extra=None):
    slots, tb, _ = tiles.shape
    width = source.shape[-1]
    smem = pl.BlockSpec(memory_space=pltpu.SMEM)
    vmem = pl.BlockSpec(memory_space=pltpu.VMEM)
    args = [target_ids, source_ids, count.reshape(1), tiles, source]
    out_rows = tb
    if extra is not None:
        args.append(extra)
        out_rows += extra.shape[0]
    return pl.pallas_call(
        functools.partial(spread_kernel, transpose),
        out_shape=jax.ShapeDtypeStruct((out_blocks, out_rows, width), out_dtype),
        in_specs=[smem, smem, smem] + [vmem] * (len(args) - 3),
        out_specs=vmem,
        scratch_shapes=[pltpu.VMEM((out_blocks, tb, width), jnp.float32)],
        cost_estimate=pl.CostEstimate(
            flops=2 * slots * tb * tb * width, transcendentals=0,
            bytes_accessed=tiles.size * 2 + source.size * 2 + out_blocks * out_rows * width * 2),
    )(*args)


def split_f32(x):
    hi = x.astype(jnp.bfloat16)
    lo = (x - hi.astype(jnp.float32)).astype(jnp.bfloat16)
    return hi, lo


def on_device(features, weight, tile_values, tile_rows, tile_cols, tile_count, cotangent):
    rows_dev = features.shape[1]
    width_in = features.shape[2]
    width_out = weight.shape[1]
    tile_size = tile_values.shape[-1]
    n_row = lax.axis_size("row")
    n_col = lax.axis_size("col")
    row_tiles = rows_dev * n_col // tile_size
    col_tiles = rows_dev * n_row // tile_size
    node_total = rows_dev * n_row * n_col
    tile_block = tile_values[0, 0]
    row_ids = tile_rows[0, 0]
    col_ids = tile_cols[0, 0]
    tile_total = tile_count[0, 0]

    own = features[0]
    gathered = lax.all_to_all(
        jnp.broadcast_to(own[None], (n_row,) + own.shape), "row", 0, 0, tiled=False
    )
    col_source = gathered.reshape(col_tiles, tile_size, width_in)
    partial_value = spread(tile_block, row_ids, col_ids, tile_total, col_source, row_tiles, False, jnp.bfloat16)
    sent = partial_value.reshape(n_col, rows_dev, width_in)
    got = lax.all_to_all(sent, "col", 0, 0, tiled=False)
    aggregated = got.astype(jnp.float32).sum(0).astype(jnp.bfloat16)

    pre = jnp.dot(aggregated, weight, preferred_element_type=jnp.float32)
    sigma = jax.nn.sigmoid(pre)
    output = (pre * sigma).astype(jnp.bfloat16)[None]
    slope = sigma * (1.0 + pre * (1.0 - sigma))
    grad_pre = (cotangent[0].astype(jnp.float32) * slope).astype(jnp.bfloat16)
    local_grad = lax.dot_general(
        aggregated, grad_pre, (((0,), (0,)), ((), ())), preferred_element_type=jnp.float32
    )
    grad_agg = lax.dot_general(
        grad_pre, weight, (((1,), (1,)), ((), ())), preferred_element_type=jnp.float32
    ).astype(jnp.bfloat16)

    wg_rows = width_in // n_col
    hi, lo = split_f32(local_grad.reshape(n_col, wg_rows, width_out))
    wg_words = jnp.stack([hi, lo], axis=1).reshape(n_col, -1, width_in)
    payload = jnp.concatenate(
        [jnp.broadcast_to(grad_agg[None], (n_col,) + grad_agg.shape), wg_words], axis=1
    )
    got = lax.all_to_all(payload, "col", 0, 0, tiled=False)
    row_source = got
    wg_got = got[:, rows_dev:].reshape(n_col, 2, wg_rows * width_out).astype(jnp.float32)
    wg_col = (wg_got[:, 0] + wg_got[:, 1]).sum(0)

    hi, lo = split_f32(wg_col)
    wg_words = jnp.stack([hi, lo]).reshape(-1, width_in)
    payload = spread(
        tile_block, col_ids, row_ids, tile_total, row_source, col_tiles, True, jnp.bfloat16, wg_words
    )
    got = lax.all_to_all(payload, "row", 0, 0, tiled=False)
    grad_features = got[:, :rows_dev].astype(jnp.float32).sum(0).astype(jnp.bfloat16)[None]
    wg_got = got[:, rows_dev:].reshape(n_row, 2, -1).astype(jnp.float32)
    wg_part = (wg_got[:, 0] + wg_got[:, 1]).sum(0) * node_total ** (-0.5)
    wg_part = wg_part.reshape(wg_rows, width_out)

    everyone = lax.all_to_all(
        jnp.broadcast_to(wg_part[None], (n_col,) + wg_part.shape), "col", 0, 0, tiled=False
    )
    weight_grad = everyone.reshape(width_in, width_out)
    return (output, grad_features, weight_grad)


def solution(mesh):
    placed = (
        P("col", "row", None),
        P(),
        P("row", "col", None, None, None),
        P("row", "col", None),
        P("row", "col", None),
        P("row", "col"),
        P("row", "col", None),
    )
    return jax.shard_map(
        on_device,
        mesh=mesh,
        in_specs=placed,
        out_specs=(P("row", "col", None), P("col", "row", None), P()),
        check_vma=False,
    )
```

```python
import functools

import jax
import jax.numpy as jnp
from jax import lax
from jax.experimental import pallas as pl
from jax.experimental.pallas import tpu as pltpu
from jax.sharding import PartitionSpec as P


def spread_kernel(transpose, rows_ref, cols_ref, count_ref, tiles_ref, src_ref, *rest):
    if len(rest) == 3:
        extra_ref, out_ref, acc_ref = rest
    else:
        extra_ref = None
        out_ref, acc_ref = rest
    tb = tiles_ref.shape[1]
    acc_ref[...] = jnp.zeros_like(acc_ref)
    live = count_ref[0]
    for t in range(tiles_ref.shape[0]):
        tile = tiles_ref[t]
        src = src_ref[cols_ref[t], :tb, :]
        if transpose:
            term = lax.dot_general(tile, src, (((0,), (0,)), ((), ())),
                                   preferred_element_type=jnp.float32)
        else:
            term = jnp.dot(tile, src, preferred_element_type=jnp.float32)
        acc_ref[rows_ref[t]] += jnp.where(t < live, term, 0.0)
    if extra_ref is None:
        out_ref[...] = acc_ref[...].astype(out_ref.dtype)
    else:
        out_ref[:, :tb, :] = acc_ref[...].astype(out_ref.dtype)
        out_ref[:, tb:, :] = jnp.broadcast_to(extra_ref[...][None], (out_ref.shape[0],) + extra_ref.shape)


def spread(tiles, target_ids, source_ids, count, source, out_blocks, transpose, out_dtype, extra=None):
    slots, tb, _ = tiles.shape
    width = source.shape[-1]
    smem = pl.BlockSpec(memory_space=pltpu.SMEM)
    vmem = pl.BlockSpec(memory_space=pltpu.VMEM)
    args = [target_ids, source_ids, count.reshape(1), tiles, source]
    out_rows = tb
    if extra is not None:
        args.append(extra)
        out_rows += extra.shape[0]
    return pl.pallas_call(
        functools.partial(spread_kernel, transpose),
        out_shape=jax.ShapeDtypeStruct((out_blocks, out_rows, width), out_dtype),
        in_specs=[smem, smem, smem] + [vmem] * (len(args) - 3),
        out_specs=vmem,
        scratch_shapes=[pltpu.VMEM((out_blocks, tb, width), jnp.float32)],
        cost_estimate=pl.CostEstimate(
            flops=2 * slots * tb * tb * width, transcendentals=0,
            bytes_accessed=tiles.size * 2 + source.size * 2 + out_blocks * out_rows * width * 2),
    )(*args)


def split_f32(x):
    hi = x.astype(jnp.bfloat16)
    lo = (x - hi.astype(jnp.float32)).astype(jnp.bfloat16)
    return hi, lo


def on_device(features, weight, tile_values, tile_rows, tile_cols, tile_count, cotangent):
    rows_dev = features.shape[1]
    width_in = features.shape[2]
    width_out = weight.shape[1]
    tile_size = tile_values.shape[-1]
    n_row = lax.axis_size("row")
    n_col = lax.axis_size("col")
    row_tiles = rows_dev * n_col // tile_size
    col_tiles = rows_dev * n_row // tile_size
    node_total = rows_dev * n_row * n_col
    tile_block = tile_values[0, 0]
    row_ids = tile_rows[0, 0]
    col_ids = tile_cols[0, 0]
    tile_total = tile_count[0, 0]

    own = features[0]
    gathered = lax.all_to_all(
        jnp.broadcast_to(own[None], (n_row,) + own.shape), "row", 0, 0, tiled=False
    )
    col_source = gathered.reshape(col_tiles, tile_size, width_in)
    partial_value = spread(tile_block, row_ids, col_ids, tile_total, col_source, row_tiles, False, jnp.bfloat16)
    sent = partial_value.reshape(n_col, rows_dev, width_in)
    got = lax.all_to_all(sent, "col", 0, 0, tiled=False)
    aggregated = got.astype(jnp.float32).sum(0).astype(jnp.bfloat16)

    pre = jnp.dot(aggregated, weight, preferred_element_type=jnp.float32)
    sigma = jax.nn.sigmoid(pre)
    output = (pre * sigma).astype(jnp.bfloat16)[None]
    slope = sigma * (1.0 + pre * (1.0 - sigma))
    grad_pre = (cotangent[0].astype(jnp.float32) * slope).astype(jnp.bfloat16)
    local_grad = lax.dot_general(
        aggregated, grad_pre, (((0,), (0,)), ((), ())), preferred_element_type=jnp.float32
    )
    grad_agg = lax.dot_general(
        grad_pre, weight, (((1,), (1,)), ((), ())), preferred_element_type=jnp.float32
    ).astype(jnp.bfloat16)

    wg_rows = width_in // n_col
    hi, lo = split_f32(local_grad.reshape(n_col, wg_rows, width_out))
    wg_words = jnp.stack([hi, lo], axis=1).reshape(n_col, -1, width_in)
    payload = jnp.concatenate(
        [jnp.broadcast_to(grad_agg[None], (n_col,) + grad_agg.shape), wg_words], axis=1
    )
    got = lax.all_to_all(payload, "col", 0, 0, tiled=False)
    row_source = got
    wg_got = got[:, rows_dev:].reshape(n_col, 2, -1, width_in).astype(jnp.float32)
    wg_col = (wg_got[:, 0] + wg_got[:, 1]).sum(0)

    hi, lo = split_f32(wg_col)
    wg_words = jnp.concatenate([hi, lo], axis=0)
    payload = spread(
        tile_block, col_ids, row_ids, tile_total, row_source, col_tiles, True, jnp.bfloat16, wg_words
    )
    got = lax.all_to_all(payload, "row", 0, 0, tiled=False)
    grad_features = got[:, :rows_dev].astype(jnp.float32).sum(0).astype(jnp.bfloat16)[None]
    wg_got = got[:, rows_dev:].reshape(n_row, 2, -1, width_in).astype(jnp.float32)
    wg_part = (wg_got[:, 0] + wg_got[:, 1]).sum(0) * node_total ** (-0.5)
    wg_part = wg_part.reshape(wg_rows, width_out)

    everyone = lax.all_to_all(
        jnp.broadcast_to(wg_part[None], (n_col,) + wg_part.shape), "col", 0, 0, tiled=False
    )
    weight_grad = everyone.reshape(width_in, width_out)
    return (output, grad_features, weight_grad)


def solution(mesh):
    placed = (
        P("col", "row", None),
        P(),
        P("row", "col", None, None, None),
        P("row", "col", None),
        P("row", "col", None),
        P("row", "col"),
        P("row", "col", None),
    )
    return jax.shard_map(
        on_device,
        mesh=mesh,
        in_specs=placed,
        out_specs=(P("row", "col", None), P("col", "row", None), P()),
        check_vma=False,
    )
```

```python
import functools

import jax
import jax.numpy as jnp
from jax import lax
from jax.experimental import pallas as pl
from jax.experimental.pallas import tpu as pltpu
from jax.sharding import PartitionSpec as P


def spread_kernel(transpose, carry_words, rows_ref, cols_ref, count_ref, tiles_ref, src_ref, out_ref, acc_ref):
    tb = tiles_ref.shape[1]
    acc_ref[...] = jnp.zeros_like(acc_ref)
    live = count_ref[0]
    for t in range(tiles_ref.shape[0]):
        tile = tiles_ref[t]
        src = src_ref[cols_ref[t], :tb, :]
        if transpose:
            term = lax.dot_general(tile, src, (((0,), (0,)), ((), ())),
                                   preferred_element_type=jnp.float32)
        else:
            term = jnp.dot(tile, src, preferred_element_type=jnp.float32)
        acc_ref[rows_ref[t]] += jnp.where(t < live, term, 0.0)
    if not carry_words:
        out_ref[...] = acc_ref[...].astype(out_ref.dtype)
    else:
        out_ref[:, :tb, :] = acc_ref[...].astype(out_ref.dtype)
        words = src_ref.shape[1] - tb
        half = words // 2
        wg = jnp.zeros((half, src_ref.shape[2]), jnp.float32)
        for j in range(src_ref.shape[0]):
            wg = wg + src_ref[j, tb:tb + half, :].astype(jnp.float32)
            wg = wg + src_ref[j, tb + half:, :].astype(jnp.float32)
        hi = wg.astype(out_ref.dtype)
        lo = (wg - hi.astype(jnp.float32)).astype(out_ref.dtype)
        for j in range(out_ref.shape[0]):
            out_ref[j, tb:tb + half, :] = hi
            out_ref[j, tb + half:, :] = lo


def spread(tiles, target_ids, source_ids, count, source, out_blocks, transpose, out_dtype, carry_words=False):
    slots, tb, _ = tiles.shape
    width = source.shape[-1]
    smem = pl.BlockSpec(memory_space=pltpu.SMEM)
    vmem = pl.BlockSpec(memory_space=pltpu.VMEM)
    args = [target_ids, source_ids, count.reshape(1), tiles, source]
    out_rows = source.shape[1] if carry_words else tb
    return pl.pallas_call(
        functools.partial(spread_kernel, transpose, carry_words),
        out_shape=jax.ShapeDtypeStruct((out_blocks, out_rows, width), out_dtype),
        in_specs=[smem, smem, smem] + [vmem] * (len(args) - 3),
        out_specs=vmem,
        scratch_shapes=[pltpu.VMEM((out_blocks, tb, width), jnp.float32)],
        cost_estimate=pl.CostEstimate(
            flops=2 * slots * tb * tb * width, transcendentals=0,
            bytes_accessed=tiles.size * 2 + source.size * 2 + out_blocks * out_rows * width * 2),
    )(*args)


def split_f32(x):
    hi = x.astype(jnp.bfloat16)
    lo = (x - hi.astype(jnp.float32)).astype(jnp.bfloat16)
    return hi, lo


def on_device(features, weight, tile_values, tile_rows, tile_cols, tile_count, cotangent):
    rows_dev = features.shape[1]
    width_in = features.shape[2]
    width_out = weight.shape[1]
    tile_size = tile_values.shape[-1]
    n_row = lax.axis_size("row")
    n_col = lax.axis_size("col")
    row_tiles = rows_dev * n_col // tile_size
    col_tiles = rows_dev * n_row // tile_size
    node_total = rows_dev * n_row * n_col
    tile_block = tile_values[0, 0]
    row_ids = tile_rows[0, 0]
    col_ids = tile_cols[0, 0]
    tile_total = tile_count[0, 0]

    own = features[0]
    gathered = lax.all_to_all(
        jnp.broadcast_to(own[None], (n_row,) + own.shape), "row", 0, 0, tiled=False
    )
    col_source = gathered.reshape(col_tiles, tile_size, width_in)
    partial_value = spread(tile_block, row_ids, col_ids, tile_total, col_source, row_tiles, False, jnp.bfloat16)
    sent = partial_value.reshape(n_col, rows_dev, width_in)
    got = lax.all_to_all(sent, "col", 0, 0, tiled=False)
    aggregated = got.astype(jnp.float32).sum(0).astype(jnp.bfloat16)

    pre = jnp.dot(aggregated, weight, preferred_element_type=jnp.float32)
    sigma = jax.nn.sigmoid(pre)
    output = (pre * sigma).astype(jnp.bfloat16)[None]
    slope = sigma * (1.0 + pre * (1.0 - sigma))
    grad_pre = (cotangent[0].astype(jnp.float32) * slope).astype(jnp.bfloat16)
    local_grad = lax.dot_general(
        aggregated, grad_pre, (((0,), (0,)), ((), ())), preferred_element_type=jnp.float32
    )
    grad_agg = lax.dot_general(
        grad_pre, weight, (((1,), (1,)), ((), ())), preferred_element_type=jnp.float32
    ).astype(jnp.bfloat16)

    wg_rows = width_in // n_col
    hi, lo = split_f32(local_grad.reshape(n_col, wg_rows, width_out))
    wg_words = jnp.concatenate(
        [hi.reshape(n_col, -1, width_in), lo.reshape(n_col, -1, width_in)], axis=1
    )
    payload = jnp.concatenate(
        [jnp.broadcast_to(grad_agg[None], (n_col,) + grad_agg.shape), wg_words], axis=1
    )
    got = lax.all_to_all(payload, "col", 0, 0, tiled=False)
    row_source = got

    payload = spread(
        tile_block, col_ids, row_ids, tile_total, row_source, col_tiles, True, jnp.bfloat16, True
    )
    got = lax.all_to_all(payload, "row", 0, 0, tiled=False)
    grad_features = got[:, :rows_dev].astype(jnp.float32).sum(0).astype(jnp.bfloat16)[None]
    wg_got = got[:, rows_dev:].reshape(n_row, 2, -1, width_in).astype(jnp.float32)
    wg_part = (wg_got[:, 0] + wg_got[:, 1]).sum(0) * node_total ** (-0.5)
    wg_part = wg_part.reshape(wg_rows, width_out)

    everyone = lax.all_to_all(
        jnp.broadcast_to(wg_part[None], (n_col,) + wg_part.shape), "col", 0, 0, tiled=False
    )
    weight_grad = everyone.reshape(width_in, width_out)
    return (output, grad_features, weight_grad)


def solution(mesh):
    placed = (
        P("col", "row", None),
        P(),
        P("row", "col", None, None, None),
        P("row", "col", None),
        P("row", "col", None),
        P("row", "col"),
        P("row", "col", None),
    )
    return jax.shard_map(
        on_device,
        mesh=mesh,
        in_specs=placed,
        out_specs=(P("row", "col", None), P("col", "row", None), P()),
        check_vma=False,
    )
```

```python
import functools

import jax
import jax.numpy as jnp
from jax import lax
from jax.experimental import pallas as pl
from jax.experimental.pallas import tpu as pltpu
from jax.sharding import PartitionSpec as P


def spread_kernel(transpose, carry_words, rows_ref, cols_ref, count_ref, tiles_ref, src_ref, out_ref, acc_ref):
    tb = tiles_ref.shape[1]
    acc_ref[...] = jnp.zeros_like(acc_ref)
    live = count_ref[0]
    n_src = src_ref.shape[0] - 1
    n_acc = acc_ref.shape[0] - 1
    for t in range(tiles_ref.shape[0]):
        tile = tiles_ref[t]
        src = src_ref[jnp.clip(cols_ref[t], 0, n_src), :tb, :]
        if transpose:
            term = lax.dot_general(tile, src, (((0,), (0,)), ((), ())),
                                   preferred_element_type=jnp.float32)
        else:
            term = jnp.dot(tile, src, preferred_element_type=jnp.float32)
        acc_ref[jnp.clip(rows_ref[t], 0, n_acc)] += jnp.where(t < live, term, 0.0)
    if not carry_words:
        out_ref[...] = acc_ref[...].astype(out_ref.dtype)
    else:
        out_ref[:, :tb, :] = acc_ref[...].astype(out_ref.dtype)
        words = src_ref.shape[1] - tb
        half = words // 2
        wg = jnp.zeros((half, src_ref.shape[2]), jnp.float32)
        for j in range(src_ref.shape[0]):
            wg = wg + src_ref[j, tb:tb + half, :].astype(jnp.float32)
            wg = wg + src_ref[j, tb + half:, :].astype(jnp.float32)
        hi = wg.astype(out_ref.dtype)
        lo = (wg - hi.astype(jnp.float32)).astype(out_ref.dtype)
        for j in range(out_ref.shape[0]):
            out_ref[j, tb:tb + half, :] = hi
            out_ref[j, tb + half:, :] = lo


def spread(tiles, target_ids, source_ids, count, source, out_blocks, transpose, out_dtype, carry_words=False):
    slots, tb, _ = tiles.shape
    width = source.shape[-1]
    smem = pl.BlockSpec(memory_space=pltpu.SMEM)
    vmem = pl.BlockSpec(memory_space=pltpu.VMEM)
    args = [target_ids, source_ids, count.reshape(1), tiles, source]
    out_rows = source.shape[1] if carry_words else tb
    return pl.pallas_call(
        functools.partial(spread_kernel, transpose, carry_words),
        out_shape=jax.ShapeDtypeStruct((out_blocks, out_rows, width), out_dtype),
        in_specs=[smem, smem, smem] + [vmem] * (len(args) - 3),
        out_specs=vmem,
        scratch_shapes=[pltpu.VMEM((out_blocks, tb, width), jnp.float32)],
        cost_estimate=pl.CostEstimate(
            flops=2 * slots * tb * tb * width, transcendentals=0,
            bytes_accessed=tiles.size * 2 + source.size * 2 + out_blocks * out_rows * width * 2),
    )(*args)


def split_f32(x):
    hi = x.astype(jnp.bfloat16)
    lo = (x - hi.astype(jnp.float32)).astype(jnp.bfloat16)
    return hi, lo


def on_device(features, weight, tile_values, tile_rows, tile_cols, tile_count, cotangent):
    rows_dev = features.shape[1]
    width_in = features.shape[2]
    width_out = weight.shape[1]
    tile_size = tile_values.shape[-1]
    n_row = lax.axis_size("row")
    n_col = lax.axis_size("col")
    row_tiles = rows_dev * n_col // tile_size
    col_tiles = rows_dev * n_row // tile_size
    node_total = rows_dev * n_row * n_col
    tile_block = tile_values[0, 0]
    row_ids = tile_rows[0, 0]
    col_ids = tile_cols[0, 0]
    tile_total = tile_count[0, 0]

    own = features[0]
    gathered = lax.all_to_all(
        jnp.broadcast_to(own[None], (n_row,) + own.shape), "row", 0, 0, tiled=False
    )
    col_source = gathered.reshape(col_tiles, tile_size, width_in)
    partial_value = spread(tile_block, row_ids, col_ids, tile_total, col_source, row_tiles, False, jnp.bfloat16)
    sent = partial_value.reshape(n_col, rows_dev, width_in)
    got = lax.all_to_all(sent, "col", 0, 0, tiled=False)
    aggregated = got.astype(jnp.float32).sum(0).astype(jnp.bfloat16)

    pre = jnp.dot(aggregated, weight, preferred_element_type=jnp.float32)
    sigma = jax.nn.sigmoid(pre)
    output = (pre * sigma).astype(jnp.bfloat16)[None]
    slope = sigma * (1.0 + pre * (1.0 - sigma))
    grad_pre = (cotangent[0].astype(jnp.float32) * slope).astype(jnp.bfloat16)
    local_grad = lax.dot_general(
        aggregated, grad_pre, (((0,), (0,)), ((), ())), preferred_element_type=jnp.float32
    )
    grad_agg = lax.dot_general(
        grad_pre, weight, (((1,), (1,)), ((), ())), preferred_element_type=jnp.float32
    ).astype(jnp.bfloat16)

    wg_rows = width_in // n_col
    hi, lo = split_f32(local_grad.reshape(n_col, wg_rows, width_out))
    wg_words = jnp.concatenate(
        [hi.reshape(n_col, -1, width_in), lo.reshape(n_col, -1, width_in)], axis=1
    )
    payload = jnp.concatenate(
        [jnp.broadcast_to(grad_agg[None], (n_col,) + grad_agg.shape), wg_words], axis=1
    )
    got = lax.all_to_all(payload, "col", 0, 0, tiled=False)
    row_source = got

    payload = spread(
        tile_block, col_ids, row_ids, tile_total, row_source, col_tiles, True, jnp.bfloat16, True
    )
    got = lax.all_to_all(payload, "row", 0, 0, tiled=False)
    grad_features = got[:, :rows_dev].astype(jnp.float32).sum(0).astype(jnp.bfloat16)[None]
    wg_got = got[:, rows_dev:].reshape(n_row, 2, -1, width_in).astype(jnp.float32)
    wg_part = (wg_got[:, 0] + wg_got[:, 1]).sum(0) * node_total ** (-0.5)
    wg_part = wg_part.reshape(wg_rows, width_out)

    everyone = lax.all_to_all(
        jnp.broadcast_to(wg_part[None], (n_col,) + wg_part.shape), "col", 0, 0, tiled=False
    )
    weight_grad = everyone.reshape(width_in, width_out)
    return (output, grad_features, weight_grad)


def solution(mesh):
    placed = (
        P("col", "row", None),
        P(),
        P("row", "col", None, None, None),
        P("row", "col", None),
        P("row", "col", None),
        P("row", "col"),
        P("row", "col", None),
    )
    return jax.shard_map(
        on_device,
        mesh=mesh,
        in_specs=placed,
        out_specs=(P("row", "col", None), P("col", "row", None), P()),
        check_vma=False,
    )
```

```python
import functools

import jax
import jax.numpy as jnp
from jax import lax
from jax.experimental import pallas as pl
from jax.experimental.pallas import tpu as pltpu
from jax.sharding import PartitionSpec as P


def spread_kernel(transpose, carry_words, chunks, rows_ref, cols_ref, count_ref, tiles_any, src_any,
                  out_ref, acc_ref, tiles_ref, src_ref, sems):
    slots = tiles_ref.shape[0]
    per = slots // chunks
    src_copy = pltpu.make_async_copy(src_any, src_ref, sems.at[chunks])
    src_copy.start()
    tile_copies = []
    for k in range(chunks):
        part = pl.ds(k * per, per)
        copy = pltpu.make_async_copy(tiles_any.at[part], tiles_ref.at[part], sems.at[k])
        copy.start()
        tile_copies.append(copy)
    tb = tiles_ref.shape[1]
    acc_ref[...] = jnp.zeros_like(acc_ref)
    live = count_ref[0]
    n_src = src_ref.shape[0] - 1
    n_acc = acc_ref.shape[0] - 1
    src_copy.wait()
    for t in range(slots):
        if t % per == 0:
            tile_copies[t // per].wait()
        tile = tiles_ref[t]
        src = src_ref[jnp.clip(cols_ref[t], 0, n_src), :tb, :]
        if transpose:
            term = lax.dot_general(tile, src, (((0,), (0,)), ((), ())),
                                   preferred_element_type=jnp.float32)
        else:
            term = jnp.dot(tile, src, preferred_element_type=jnp.float32)
        acc_ref[jnp.clip(rows_ref[t], 0, n_acc)] += jnp.where(t < live, term, 0.0)
    if not carry_words:
        out_ref[...] = acc_ref[...].astype(out_ref.dtype)
    else:
        out_ref[:, :tb, :] = acc_ref[...].astype(out_ref.dtype)
        words = src_ref.shape[1] - tb
        half = words // 2
        wg = jnp.zeros((half, src_ref.shape[2]), jnp.float32)
        for j in range(src_ref.shape[0]):
            wg = wg + src_ref[j, tb:tb + half, :].astype(jnp.float32)
            wg = wg + src_ref[j, tb + half:, :].astype(jnp.float32)
        hi = wg.astype(out_ref.dtype)
        lo = (wg - hi.astype(jnp.float32)).astype(out_ref.dtype)
        for j in range(out_ref.shape[0]):
            out_ref[j, tb:tb + half, :] = hi
            out_ref[j, tb + half:, :] = lo


def spread(tiles, target_ids, source_ids, count, source, out_blocks, transpose, out_dtype, carry_words=False):
    slots, tb, _ = tiles.shape
    chunks = 4 if slots % 4 == 0 else 1
    width = source.shape[-1]
    smem = pl.BlockSpec(memory_space=pltpu.SMEM)
    vmem = pl.BlockSpec(memory_space=pltpu.VMEM)
    args = [target_ids, source_ids, count.reshape(1), tiles, source]
    out_rows = source.shape[1] if carry_words else tb
    return pl.pallas_call(
        functools.partial(spread_kernel, transpose, carry_words, chunks),
        out_shape=jax.ShapeDtypeStruct((out_blocks, out_rows, width), out_dtype),
        in_specs=[smem, smem, smem, pl.BlockSpec(memory_space=pl.ANY), pl.BlockSpec(memory_space=pl.ANY)],
        out_specs=vmem,
        scratch_shapes=[
            pltpu.VMEM((out_blocks, tb, width), jnp.float32),
            pltpu.VMEM(tiles.shape, tiles.dtype),
            pltpu.VMEM(source.shape, source.dtype),
            pltpu.SemaphoreType.DMA((chunks + 1,)),
        ],
        cost_estimate=pl.CostEstimate(
            flops=2 * slots * tb * tb * width, transcendentals=0,
            bytes_accessed=tiles.size * 2 + source.size * 2 + out_blocks * out_rows * width * 2),
    )(*args)


def split_f32(x):
    hi = x.astype(jnp.bfloat16)
    lo = (x - hi.astype(jnp.float32)).astype(jnp.bfloat16)
    return hi, lo


def on_device(features, weight, tile_values, tile_rows, tile_cols, tile_count, cotangent):
    rows_dev = features.shape[1]
    width_in = features.shape[2]
    width_out = weight.shape[1]
    tile_size = tile_values.shape[-1]
    n_row = lax.axis_size("row")
    n_col = lax.axis_size("col")
    row_tiles = rows_dev * n_col // tile_size
    col_tiles = rows_dev * n_row // tile_size
    node_total = rows_dev * n_row * n_col
    tile_block = tile_values[0, 0]
    row_ids = tile_rows[0, 0]
    col_ids = tile_cols[0, 0]
    tile_total = tile_count[0, 0]

    own = features[0]
    gathered = lax.all_to_all(
        jnp.broadcast_to(own[None], (n_row,) + own.shape), "row", 0, 0, tiled=False
    )
    col_source = gathered.reshape(col_tiles, tile_size, width_in)
    partial_value = spread(tile_block, row_ids, col_ids, tile_total, col_source, row_tiles, False, jnp.bfloat16)
    sent = partial_value.reshape(n_col, rows_dev, width_in)
    got = lax.all_to_all(sent, "col", 0, 0, tiled=False)
    aggregated = got.astype(jnp.float32).sum(0).astype(jnp.bfloat16)

    pre = jnp.dot(aggregated, weight, preferred_element_type=jnp.float32)
    sigma = jax.nn.sigmoid(pre)
    output = (pre * sigma).astype(jnp.bfloat16)[None]
    slope = sigma * (1.0 + pre * (1.0 - sigma))
    grad_pre = (cotangent[0].astype(jnp.float32) * slope).astype(jnp.bfloat16)
    local_grad = lax.dot_general(
        aggregated, grad_pre, (((0,), (0,)), ((), ())), preferred_element_type=jnp.float32
    )
    grad_agg = lax.dot_general(
        grad_pre, weight, (((1,), (1,)), ((), ())), preferred_element_type=jnp.float32
    ).astype(jnp.bfloat16)

    wg_rows = width_in // n_col
    hi, lo = split_f32(local_grad.reshape(n_col, wg_rows, width_out))
    wg_words = jnp.concatenate(
        [hi.reshape(n_col, -1, width_in), lo.reshape(n_col, -1, width_in)], axis=1
    )
    payload = jnp.concatenate(
        [jnp.broadcast_to(grad_agg[None], (n_col,) + grad_agg.shape), wg_words], axis=1
    )
    got = lax.all_to_all(payload, "col", 0, 0, tiled=False)
    row_source = got

    payload = spread(
        tile_block, col_ids, row_ids, tile_total, row_source, col_tiles, True, jnp.bfloat16, True
    )
    got = lax.all_to_all(payload, "row", 0, 0, tiled=False)
    grad_features = got[:, :rows_dev].astype(jnp.float32).sum(0).astype(jnp.bfloat16)[None]
    wg_got = got[:, rows_dev:].reshape(n_row, 2, -1, width_in).astype(jnp.float32)
    wg_part = (wg_got[:, 0] + wg_got[:, 1]).sum(0) * node_total ** (-0.5)
    wg_part = wg_part.reshape(wg_rows, width_out)

    everyone = lax.all_to_all(
        jnp.broadcast_to(wg_part[None], (n_col,) + wg_part.shape), "col", 0, 0, tiled=False
    )
    weight_grad = everyone.reshape(width_in, width_out)
    return (output, grad_features, weight_grad)


def solution(mesh):
    placed = (
        P("col", "row", None),
        P(),
        P("row", "col", None, None, None),
        P("row", "col", None),
        P("row", "col", None),
        P("row", "col"),
        P("row", "col", None),
    )
    return jax.shard_map(
        on_device,
        mesh=mesh,
        in_specs=placed,
        out_specs=(P("row", "col", None), P("col", "row", None), P()),
        check_vma=False,
    )
```

```python
import functools

import jax
import jax.numpy as jnp
from jax import lax
from jax.experimental import pallas as pl
from jax.experimental.pallas import tpu as pltpu
from jax.sharding import PartitionSpec as P


def spread_kernel(transpose, carry_words, rows_ref, cols_ref, count_ref, tiles_ref, src_ref, out_ref, acc_ref):
    tb = tiles_ref.shape[1]
    acc_ref[...] = jnp.zeros_like(acc_ref)
    live = count_ref[0]
    n_src = src_ref.shape[0] - 1
    n_acc = acc_ref.shape[0] - 1
    for t in range(tiles_ref.shape[0]):
        tile = tiles_ref[t]
        src = src_ref[jnp.clip(cols_ref[t], 0, n_src), :tb, :]
        if transpose:
            term = lax.dot_general(tile, src, (((0,), (0,)), ((), ())),
                                   preferred_element_type=jnp.float32)
        else:
            term = jnp.dot(tile, src, preferred_element_type=jnp.float32)
        acc_ref[jnp.clip(rows_ref[t], 0, n_acc)] += jnp.where(t < live, term, 0.0)
    if not carry_words:
        out_ref[...] = acc_ref[...].astype(out_ref.dtype)
    else:
        out_ref[:, :tb, :] = acc_ref[...].astype(out_ref.dtype)
        wg = jnp.zeros((src_ref.shape[1] - tb, src_ref.shape[2]), jnp.float32)
        for j in range(src_ref.shape[0]):
            wg = wg + src_ref[j, tb:, :].astype(jnp.float32)
        words = wg.astype(out_ref.dtype)
        for j in range(out_ref.shape[0]):
            out_ref[j, tb:, :] = words


def spread(tiles, target_ids, source_ids, count, source, out_blocks, transpose, out_dtype, carry_words=False):
    slots, tb, _ = tiles.shape
    width = source.shape[-1]
    smem = pl.BlockSpec(memory_space=pltpu.SMEM)
    vmem = pl.BlockSpec(memory_space=pltpu.VMEM)
    args = [target_ids, source_ids, count.reshape(1), tiles, source]
    out_rows = source.shape[1] if carry_words else tb
    return pl.pallas_call(
        functools.partial(spread_kernel, transpose, carry_words),
        out_shape=jax.ShapeDtypeStruct((out_blocks, out_rows, width), out_dtype),
        in_specs=[smem, smem, smem] + [vmem] * (len(args) - 3),
        out_specs=vmem,
        scratch_shapes=[pltpu.VMEM((out_blocks, tb, width), jnp.float32)],
        cost_estimate=pl.CostEstimate(
            flops=2 * slots * tb * tb * width, transcendentals=0,
            bytes_accessed=tiles.size * 2 + source.size * 2 + out_blocks * out_rows * width * 2),
    )(*args)


def on_device(features, weight, tile_values, tile_rows, tile_cols, tile_count, cotangent):
    rows_dev = features.shape[1]
    width_in = features.shape[2]
    width_out = weight.shape[1]
    tile_size = tile_values.shape[-1]
    n_row = lax.axis_size("row")
    n_col = lax.axis_size("col")
    row_tiles = rows_dev * n_col // tile_size
    col_tiles = rows_dev * n_row // tile_size
    node_total = rows_dev * n_row * n_col
    tile_block = tile_values[0, 0]
    row_ids = tile_rows[0, 0]
    col_ids = tile_cols[0, 0]
    tile_total = tile_count[0, 0]

    own = features[0]
    gathered = lax.all_to_all(
        jnp.broadcast_to(own[None], (n_row,) + own.shape), "row", 0, 0, tiled=False
    )
    col_source = gathered.reshape(col_tiles, tile_size, width_in)
    partial_value = spread(tile_block, row_ids, col_ids, tile_total, col_source, row_tiles, False, jnp.bfloat16)
    sent = partial_value.reshape(n_col, rows_dev, width_in)
    got = lax.all_to_all(sent, "col", 0, 0, tiled=False)
    aggregated = got.astype(jnp.float32).sum(0).astype(jnp.bfloat16)

    pre = jnp.dot(aggregated, weight, preferred_element_type=jnp.float32)
    sigma = jax.nn.sigmoid(pre)
    output = (pre * sigma).astype(jnp.bfloat16)[None]
    slope = sigma * (1.0 + pre * (1.0 - sigma))
    grad_pre = (cotangent[0].astype(jnp.float32) * slope).astype(jnp.bfloat16)
    local_grad = lax.dot_general(
        aggregated, grad_pre, (((0,), (0,)), ((), ())), preferred_element_type=jnp.float32
    )
    grad_agg = lax.dot_general(
        grad_pre, weight, (((1,), (1,)), ((), ())), preferred_element_type=jnp.float32
    ).astype(jnp.bfloat16)

    wg_rows = width_in // n_col
    wg_words = local_grad.reshape(n_col, -1, width_in).astype(jnp.bfloat16)
    payload = jnp.concatenate(
        [jnp.broadcast_to(grad_agg[None], (n_col,) + grad_agg.shape), wg_words], axis=1
    )
    got = lax.all_to_all(payload, "col", 0, 0, tiled=False)
    row_source = got

    payload = spread(
        tile_block, col_ids, row_ids, tile_total, row_source, col_tiles, True, jnp.bfloat16, True
    )
    got = lax.all_to_all(payload, "row", 0, 0, tiled=False)
    grad_features = got[:, :rows_dev].astype(jnp.float32).sum(0).astype(jnp.bfloat16)[None]
    wg_part = got[:, rows_dev:].astype(jnp.float32).sum(0) * node_total ** (-0.5)
    wg_part = wg_part.reshape(wg_rows, width_out)

    everyone = lax.all_to_all(
        jnp.broadcast_to(wg_part[None], (n_col,) + wg_part.shape), "col", 0, 0, tiled=False
    )
    weight_grad = everyone.reshape(width_in, width_out)
    return (output, grad_features, weight_grad)


def solution(mesh):
    placed = (
        P("col", "row", None),
        P(),
        P("row", "col", None, None, None),
        P("row", "col", None),
        P("row", "col", None),
        P("row", "col"),
        P("row", "col", None),
    )
    return jax.shard_map(
        on_device,
        mesh=mesh,
        in_specs=placed,
        out_specs=(P("row", "col", None), P("col", "row", None), P()),
        check_vma=False,
    )
```

```python
import functools

import jax
import jax.numpy as jnp
from jax import lax
from jax.experimental import pallas as pl
from jax.experimental.pallas import tpu as pltpu
from jax.sharding import PartitionSpec as P


def spread_kernel(transpose, carry_words, rows_ref, cols_ref, count_ref, tiles_ref, src_ref, out_ref, acc_ref):
    tb = tiles_ref.shape[1]
    acc_ref[...] = jnp.zeros_like(acc_ref)
    live = count_ref[0]
    n_src = src_ref.shape[0] - 1
    n_acc = acc_ref.shape[0] - 1
    slots = tiles_ref.shape[0]
    group = 2 if slots % 2 == 0 else 1
    for first in range(0, slots, group):
        terms = []
        for t in range(first, first + group):
            tile = tiles_ref[t]
            src = src_ref[jnp.clip(cols_ref[t], 0, n_src), :tb, :]
            if transpose:
                term = lax.dot_general(tile, src, (((0,), (0,)), ((), ())),
                                       preferred_element_type=jnp.float32)
            else:
                term = jnp.dot(tile, src, preferred_element_type=jnp.float32)
            terms.append(jnp.where(t < live, term, 0.0))
        for t, term in zip(range(first, first + group), terms):
            acc_ref[jnp.clip(rows_ref[t], 0, n_acc)] += term
    if not carry_words:
        out_ref[...] = acc_ref[...].astype(out_ref.dtype)
    else:
        out_ref[:, :tb, :] = acc_ref[...].astype(out_ref.dtype)
        wg = jnp.zeros((src_ref.shape[1] - tb, src_ref.shape[2]), jnp.float32)
        for j in range(src_ref.shape[0]):
            wg = wg + src_ref[j, tb:, :].astype(jnp.float32)
        words = wg.astype(out_ref.dtype)
        for j in range(out_ref.shape[0]):
            out_ref[j, tb:, :] = words


def spread(tiles, target_ids, source_ids, count, source, out_blocks, transpose, out_dtype, carry_words=False):
    slots, tb, _ = tiles.shape
    width = source.shape[-1]
    smem = pl.BlockSpec(memory_space=pltpu.SMEM)
    vmem = pl.BlockSpec(memory_space=pltpu.VMEM)
    args = [target_ids, source_ids, count.reshape(1), tiles, source]
    out_rows = source.shape[1] if carry_words else tb
    return pl.pallas_call(
        functools.partial(spread_kernel, transpose, carry_words),
        out_shape=jax.ShapeDtypeStruct((out_blocks, out_rows, width), out_dtype),
        in_specs=[smem, smem, smem] + [vmem] * (len(args) - 3),
        out_specs=vmem,
        scratch_shapes=[pltpu.VMEM((out_blocks, tb, width), jnp.float32)],
        cost_estimate=pl.CostEstimate(
            flops=2 * slots * tb * tb * width, transcendentals=0,
            bytes_accessed=tiles.size * 2 + source.size * 2 + out_blocks * out_rows * width * 2),
    )(*args)


def on_device(features, weight, tile_values, tile_rows, tile_cols, tile_count, cotangent):
    rows_dev = features.shape[1]
    width_in = features.shape[2]
    width_out = weight.shape[1]
    tile_size = tile_values.shape[-1]
    n_row = lax.axis_size("row")
    n_col = lax.axis_size("col")
    row_tiles = rows_dev * n_col // tile_size
    col_tiles = rows_dev * n_row // tile_size
    node_total = rows_dev * n_row * n_col
    tile_block = tile_values[0, 0]
    row_ids = tile_rows[0, 0]
    col_ids = tile_cols[0, 0]
    tile_total = tile_count[0, 0]

    own = features[0]
    gathered = lax.all_to_all(
        jnp.broadcast_to(own[None], (n_row,) + own.shape), "row", 0, 0, tiled=False
    )
    col_source = gathered.reshape(col_tiles, tile_size, width_in)
    partial_value = spread(tile_block, row_ids, col_ids, tile_total, col_source, row_tiles, False, jnp.bfloat16)
    sent = partial_value.reshape(n_col, rows_dev, width_in)
    got = lax.all_to_all(sent, "col", 0, 0, tiled=False)
    aggregated = got.astype(jnp.float32).sum(0).astype(jnp.bfloat16)

    pre = jnp.dot(aggregated, weight, preferred_element_type=jnp.float32)
    sigma = jax.nn.sigmoid(pre)
    output = (pre * sigma).astype(jnp.bfloat16)[None]
    slope = sigma * (1.0 + pre * (1.0 - sigma))
    grad_pre = (cotangent[0].astype(jnp.float32) * slope).astype(jnp.bfloat16)
    local_grad = lax.dot_general(
        aggregated, grad_pre, (((0,), (0,)), ((), ())), preferred_element_type=jnp.float32
    )
    grad_agg = lax.dot_general(
        grad_pre, weight, (((1,), (1,)), ((), ())), preferred_element_type=jnp.float32
    ).astype(jnp.bfloat16)

    wg_rows = width_in // n_col
    wg_words = local_grad.reshape(n_col, -1, width_in).astype(jnp.bfloat16)
    payload = jnp.concatenate(
        [jnp.broadcast_to(grad_agg[None], (n_col,) + grad_agg.shape), wg_words], axis=1
    )
    got = lax.all_to_all(payload, "col", 0, 0, tiled=False)
    row_source = got

    payload = spread(
        tile_block, col_ids, row_ids, tile_total, row_source, col_tiles, True, jnp.bfloat16, True
    )
    got = lax.all_to_all(payload, "row", 0, 0, tiled=False)
    grad_features = got[:, :rows_dev].astype(jnp.float32).sum(0).astype(jnp.bfloat16)[None]
    wg_part = got[:, rows_dev:].astype(jnp.float32).sum(0) * node_total ** (-0.5)
    wg_part = wg_part.reshape(wg_rows, width_out)

    everyone = lax.all_to_all(
        jnp.broadcast_to(wg_part[None], (n_col,) + wg_part.shape), "col", 0, 0, tiled=False
    )
    weight_grad = everyone.reshape(width_in, width_out)
    return (output, grad_features, weight_grad)


def solution(mesh):
    placed = (
        P("col", "row", None),
        P(),
        P("row", "col", None, None, None),
        P("row", "col", None),
        P("row", "col", None),
        P("row", "col"),
        P("row", "col", None),
    )
    return jax.shard_map(
        on_device,
        mesh=mesh,
        in_specs=placed,
        out_specs=(P("row", "col", None), P("col", "row", None), P()),
        check_vma=False,
    )
```

```python
import functools

import jax
import jax.numpy as jnp
from jax import lax
from jax.experimental import pallas as pl
from jax.experimental.pallas import tpu as pltpu
from jax.sharding import PartitionSpec as P


def spread_kernel(transpose, carry_words, rows_ref, cols_ref, count_ref, tiles_ref, src_ref, out_ref, acc_ref):
    tb = tiles_ref.shape[1]
    acc_ref[...] = jnp.zeros_like(acc_ref)
    live = count_ref[0]
    n_src = src_ref.shape[0] - 1
    n_acc = acc_ref.shape[0] - 1
    slots = tiles_ref.shape[0]
    group = 2 if slots % 2 == 0 else 1
    for first in range(0, slots, group):
        terms = []
        for t in range(first, first + group):
            tile = tiles_ref[t]
            src = src_ref[jnp.clip(cols_ref[t], 0, n_src), :tb, :]
            if transpose:
                term = lax.dot_general(tile, src, (((0,), (0,)), ((), ())),
                                       preferred_element_type=jnp.float32)
            else:
                term = jnp.dot(tile, src, preferred_element_type=jnp.float32)
            terms.append(jnp.where(t < live, term, 0.0))
        for t, term in zip(range(first, first + group), terms):
            acc_ref[jnp.clip(rows_ref[t], 0, n_acc)] += term
    if not carry_words:
        out_ref[...] = acc_ref[...].astype(out_ref.dtype)
    else:
        out_ref[:, :tb, :] = acc_ref[...].astype(out_ref.dtype)
        wg = jnp.zeros((src_ref.shape[1] - tb, src_ref.shape[2]), jnp.float32)
        for j in range(src_ref.shape[0]):
            wg = wg + src_ref[j, tb:, :].astype(jnp.float32)
        words = wg.astype(out_ref.dtype)
        for j in range(out_ref.shape[0]):
            out_ref[j, tb:, :] = words


def spread(tiles, target_ids, source_ids, count, source, out_blocks, transpose, out_dtype, carry_words=False):
    slots, tb, _ = tiles.shape
    width = source.shape[-1]
    smem = pl.BlockSpec(memory_space=pltpu.SMEM)
    vmem = pl.BlockSpec(memory_space=pltpu.VMEM)
    args = [target_ids, source_ids, count.reshape(1), tiles, source]
    out_rows = source.shape[1] if carry_words else tb
    return pl.pallas_call(
        functools.partial(spread_kernel, transpose, carry_words),
        out_shape=jax.ShapeDtypeStruct((out_blocks, out_rows, width), out_dtype),
        in_specs=[smem, smem, smem] + [vmem] * (len(args) - 3),
        out_specs=vmem,
        scratch_shapes=[pltpu.VMEM((out_blocks, tb, width), jnp.float32)],
        cost_estimate=pl.CostEstimate(
            flops=2 * slots * tb * tb * width, transcendentals=0,
            bytes_accessed=tiles.size * 2 + source.size * 2 + out_blocks * out_rows * width * 2),
    )(*args)


def dense_kernel(recv_ref, w_ref, cot_ref, out_ref, pay_ref):
    agg = recv_ref[...].astype(jnp.float32).sum(0).astype(jnp.bfloat16)
    weight = w_ref[...]
    pre = jnp.dot(agg, weight, preferred_element_type=jnp.float32)
    sigma = jax.nn.sigmoid(pre)
    out_ref[...] = (pre * sigma).astype(out_ref.dtype)
    slope = sigma * (1.0 + pre * (1.0 - sigma))
    grad_pre = (cot_ref[...].astype(jnp.float32) * slope).astype(jnp.bfloat16)
    local_grad = lax.dot_general(agg, grad_pre, (((0,), (0,)), ((), ())),
                                 preferred_element_type=jnp.float32)
    grad_agg = lax.dot_general(grad_pre, weight, (((1,), (1,)), ((), ())),
                               preferred_element_type=jnp.float32).astype(pay_ref.dtype)
    tb = grad_agg.shape[0]
    blocks = pay_ref.shape[0]
    rows = local_grad.shape[0] // blocks
    half = local_grad.shape[1] // 2
    for j in range(blocks):
        pay_ref[j, :tb, :] = grad_agg
        part = local_grad[j * rows:(j + 1) * rows, :].astype(pay_ref.dtype)
        pay_ref[j, tb:tb + rows, :] = part[:, :half]
        pay_ref[j, tb + rows:tb + 2 * rows, :] = part[:, half:]


def dense(recv, weight, cot):
    blocks, tb, width_in = recv.shape
    width_out = weight.shape[1]
    rows = width_in // blocks
    vmem = pl.BlockSpec(memory_space=pltpu.VMEM)
    return pl.pallas_call(
        dense_kernel,
        out_shape=(
            jax.ShapeDtypeStruct((tb, width_out), jnp.bfloat16),
            jax.ShapeDtypeStruct((blocks, tb + 2 * rows, width_in), jnp.bfloat16),
        ),
        in_specs=[vmem, vmem, vmem],
        out_specs=(vmem, vmem),
        cost_estimate=pl.CostEstimate(
            flops=6 * tb * width_in * width_out, transcendentals=tb * width_out,
            bytes_accessed=recv.size * 2 + weight.size * 2 + cot.size * 2 + tb * width_out * 2
            + blocks * (tb + 2 * rows) * width_in * 2),
    )(recv, weight, cot)


def on_device(features, weight, tile_values, tile_rows, tile_cols, tile_count, cotangent):
    rows_dev = features.shape[1]
    width_in = features.shape[2]
    width_out = weight.shape[1]
    tile_size = tile_values.shape[-1]
    n_row = lax.axis_size("row")
    n_col = lax.axis_size("col")
    row_tiles = rows_dev * n_col // tile_size
    col_tiles = rows_dev * n_row // tile_size
    node_total = rows_dev * n_row * n_col
    tile_block = tile_values[0, 0]
    row_ids = tile_rows[0, 0]
    col_ids = tile_cols[0, 0]
    tile_total = tile_count[0, 0]

    own = features[0]
    gathered = lax.all_to_all(
        jnp.broadcast_to(own[None], (n_row,) + own.shape), "row", 0, 0, tiled=False
    )
    col_source = gathered.reshape(col_tiles, tile_size, width_in)
    partial_value = spread(tile_block, row_ids, col_ids, tile_total, col_source, row_tiles, False, jnp.bfloat16)
    sent = partial_value.reshape(n_col, rows_dev, width_in)
    got = lax.all_to_all(sent, "col", 0, 0, tiled=False)
    out_block, payload = dense(got, weight, cotangent[0])
    output = out_block[None]
    wg_rows = width_in // n_col
    got = lax.all_to_all(payload, "col", 0, 0, tiled=False)
    row_source = got

    payload = spread(
        tile_block, col_ids, row_ids, tile_total, row_source, col_tiles, True, jnp.bfloat16, True
    )
    got = lax.all_to_all(payload, "row", 0, 0, tiled=False)
    grad_features = got[:, :rows_dev].astype(jnp.float32).sum(0).astype(jnp.bfloat16)[None]
    wg_part = got[:, rows_dev:].astype(jnp.float32).sum(0) * node_total ** (-0.5)
    wg_part = wg_part.reshape(2, wg_rows, width_in).transpose(1, 0, 2).reshape(wg_rows, width_out)

    everyone = lax.all_to_all(
        jnp.broadcast_to(wg_part[None], (n_col,) + wg_part.shape), "col", 0, 0, tiled=False
    )
    weight_grad = everyone.reshape(width_in, width_out)
    return (output, grad_features, weight_grad)


def solution(mesh):
    placed = (
        P("col", "row", None),
        P(),
        P("row", "col", None, None, None),
        P("row", "col", None),
        P("row", "col", None),
        P("row", "col"),
        P("row", "col", None),
    )
    return jax.shard_map(
        on_device,
        mesh=mesh,
        in_specs=placed,
        out_specs=(P("row", "col", None), P("col", "row", None), P()),
        check_vma=False,
    )
```

```python
import functools

import jax
import jax.numpy as jnp
from jax import lax
from jax.experimental import pallas as pl
from jax.experimental.pallas import tpu as pltpu
from jax.sharding import PartitionSpec as P


def spread_kernel(transpose, carry_words, rows_ref, cols_ref, count_ref, tiles_ref, src_ref, out_ref, acc_ref):
    tb = tiles_ref.shape[1]
    acc_ref[...] = jnp.zeros_like(acc_ref)
    live = count_ref[0]
    n_src = src_ref.shape[0] - 1
    n_acc = acc_ref.shape[0] - 1
    slots = tiles_ref.shape[0]
    group = 2 if slots % 2 == 0 else 1
    for first in range(0, slots, group):
        terms = []
        for t in range(first, first + group):
            tile = tiles_ref[t]
            src = src_ref[jnp.clip(cols_ref[t], 0, n_src), :tb, :]
            if transpose:
                term = lax.dot_general(tile, src, (((0,), (0,)), ((), ())),
                                       preferred_element_type=jnp.float32)
            else:
                term = jnp.dot(tile, src, preferred_element_type=jnp.float32)
            terms.append(jnp.where(t < live, term, 0.0))
        for t, term in zip(range(first, first + group), terms):
            acc_ref[jnp.clip(rows_ref[t], 0, n_acc)] += term
    if not carry_words:
        out_ref[...] = acc_ref[...].astype(out_ref.dtype)
    else:
        out_ref[:, :tb, :] = acc_ref[...].astype(out_ref.dtype)
        wg = jnp.zeros((src_ref.shape[1] - tb, src_ref.shape[2]), jnp.float32)
        for j in range(src_ref.shape[0]):
            wg = wg + src_ref[j, tb:, :].astype(jnp.float32)
        words = wg.astype(out_ref.dtype)
        for j in range(out_ref.shape[0]):
            out_ref[j, tb:, :] = words


def spread(tiles, target_ids, source_ids, count, source, out_blocks, transpose, out_dtype, carry_words=False):
    slots, tb, _ = tiles.shape
    width = source.shape[-1]
    smem = pl.BlockSpec(memory_space=pltpu.SMEM)
    vmem = pl.BlockSpec(memory_space=pltpu.VMEM)
    tiles = pltpu.with_memory_space_constraint(tiles, pltpu.VMEM)
    source = pltpu.with_memory_space_constraint(source, pltpu.VMEM)
    args = [target_ids, source_ids, count.reshape(1), tiles, source]
    out_rows = source.shape[1] if carry_words else tb
    return pl.pallas_call(
        functools.partial(spread_kernel, transpose, carry_words),
        out_shape=jax.ShapeDtypeStruct((out_blocks, out_rows, width), out_dtype),
        in_specs=[smem, smem, smem] + [vmem] * (len(args) - 3),
        out_specs=vmem,
        scratch_shapes=[pltpu.VMEM((out_blocks, tb, width), jnp.float32)],
        cost_estimate=pl.CostEstimate(
            flops=2 * slots * tb * tb * width, transcendentals=0,
            bytes_accessed=tiles.size * 2 + source.size * 2 + out_blocks * out_rows * width * 2),
    )(*args)


def on_device(features, weight, tile_values, tile_rows, tile_cols, tile_count, cotangent):
    rows_dev = features.shape[1]
    width_in = features.shape[2]
    width_out = weight.shape[1]
    tile_size = tile_values.shape[-1]
    n_row = lax.axis_size("row")
    n_col = lax.axis_size("col")
    row_tiles = rows_dev * n_col // tile_size
    col_tiles = rows_dev * n_row // tile_size
    node_total = rows_dev * n_row * n_col
    tile_block = tile_values[0, 0]
    row_ids = tile_rows[0, 0]
    col_ids = tile_cols[0, 0]
    tile_total = tile_count[0, 0]

    own = features[0]
    gathered = lax.all_to_all(
        jnp.broadcast_to(own[None], (n_row,) + own.shape), "row", 0, 0, tiled=False
    )
    col_source = gathered.reshape(col_tiles, tile_size, width_in)
    partial_value = spread(tile_block, row_ids, col_ids, tile_total, col_source, row_tiles, False, jnp.bfloat16)
    sent = partial_value.reshape(n_col, rows_dev, width_in)
    got = lax.all_to_all(sent, "col", 0, 0, tiled=False)
    aggregated = got.astype(jnp.float32).sum(0).astype(jnp.bfloat16)

    pre = jnp.dot(aggregated, weight, preferred_element_type=jnp.float32)
    sigma = jax.nn.sigmoid(pre)
    output = (pre * sigma).astype(jnp.bfloat16)[None]
    slope = sigma * (1.0 + pre * (1.0 - sigma))
    grad_pre = (cotangent[0].astype(jnp.float32) * slope).astype(jnp.bfloat16)
    local_grad = lax.dot_general(
        aggregated, grad_pre, (((0,), (0,)), ((), ())), preferred_element_type=jnp.float32
    )
    grad_agg = lax.dot_general(
        grad_pre, weight, (((1,), (1,)), ((), ())), preferred_element_type=jnp.float32
    ).astype(jnp.bfloat16)

    wg_rows = width_in // n_col
    wg_words = local_grad.reshape(n_col, -1, width_in).astype(jnp.bfloat16)
    payload = jnp.concatenate(
        [jnp.broadcast_to(grad_agg[None], (n_col,) + grad_agg.shape), wg_words], axis=1
    )
    got = lax.all_to_all(payload, "col", 0, 0, tiled=False)
    row_source = got

    payload = spread(
        tile_block, col_ids, row_ids, tile_total, row_source, col_tiles, True, jnp.bfloat16, True
    )
    got = lax.all_to_all(payload, "row", 0, 0, tiled=False)
    grad_features = got[:, :rows_dev].astype(jnp.float32).sum(0).astype(jnp.bfloat16)[None]
    wg_part = got[:, rows_dev:].astype(jnp.float32).sum(0) * node_total ** (-0.5)
    wg_part = wg_part.reshape(wg_rows, width_out)

    everyone = lax.all_to_all(
        jnp.broadcast_to(wg_part[None], (n_col,) + wg_part.shape), "col", 0, 0, tiled=False
    )
    weight_grad = everyone.reshape(width_in, width_out)
    return (output, grad_features, weight_grad)


def solution(mesh):
    placed = (
        P("col", "row", None),
        P(),
        P("row", "col", None, None, None),
        P("row", "col", None),
        P("row", "col", None),
        P("row", "col"),
        P("row", "col", None),
    )
    return jax.shard_map(
        on_device,
        mesh=mesh,
        in_specs=placed,
        out_specs=(P("row", "col", None), P("col", "row", None), P()),
        check_vma=False,
    )
```

```python
import functools

import jax
import jax.numpy as jnp
from jax import lax
from jax.experimental import pallas as pl
from jax.experimental.pallas import tpu as pltpu
from jax.sharding import PartitionSpec as P


def spread_kernel(transpose, carry_words, rows_ref, cols_ref, count_ref, tiles_ref, src_ref, out_ref, acc_ref):
    tb = tiles_ref.shape[1]
    acc_ref[...] = jnp.zeros_like(acc_ref)
    live = count_ref[0]
    n_src = src_ref.shape[0] - 1
    n_acc = acc_ref.shape[0] - 1
    slots = tiles_ref.shape[0]
    group = 2 if slots % 2 == 0 else 1
    for first in range(0, slots, group):
        terms = []
        for t in range(first, first + group):
            tile = tiles_ref[t]
            src = src_ref[jnp.clip(cols_ref[t], 0, n_src), :tb, :]
            if transpose:
                term = lax.dot_general(tile, src, (((0,), (0,)), ((), ())),
                                       preferred_element_type=jnp.float32)
            else:
                term = jnp.dot(tile, src, preferred_element_type=jnp.float32)
            terms.append(jnp.where(t < live, term, 0.0))
        for t, term in zip(range(first, first + group), terms):
            acc_ref[jnp.clip(rows_ref[t], 0, n_acc)] += term
    if not carry_words:
        out_ref[...] = acc_ref[...].astype(out_ref.dtype)
    else:
        out_ref[:, :tb, :] = acc_ref[...].astype(out_ref.dtype)
        wg = jnp.zeros((src_ref.shape[1] - tb, src_ref.shape[2]), jnp.float32)
        for j in range(src_ref.shape[0]):
            wg = wg + src_ref[j, tb:, :].astype(jnp.float32)
        words = wg.astype(out_ref.dtype)
        for j in range(out_ref.shape[0]):
            out_ref[j, tb:, :] = words


def spread(tiles, target_ids, source_ids, count, source, out_blocks, transpose, out_dtype, carry_words=False):
    slots, tb, _ = tiles.shape
    width = source.shape[-1]
    smem = pl.BlockSpec(memory_space=pltpu.SMEM)
    vmem = pl.BlockSpec(memory_space=pltpu.VMEM)
    tiles = pltpu.with_memory_space_constraint(tiles, pltpu.VMEM)
    source = pltpu.with_memory_space_constraint(source, pltpu.VMEM)
    args = [target_ids, source_ids, count.reshape(1), tiles, source]
    out_rows = source.shape[1] if carry_words else tb
    return pl.pallas_call(
        functools.partial(spread_kernel, transpose, carry_words),
        out_shape=jax.ShapeDtypeStruct((out_blocks, out_rows, width), out_dtype),
        in_specs=[smem, smem, smem] + [vmem] * (len(args) - 3),
        out_specs=vmem,
        scratch_shapes=[pltpu.VMEM((out_blocks, tb, width), jnp.float32)],
        cost_estimate=pl.CostEstimate(
            flops=2 * slots * tb * tb * width, transcendentals=0,
            bytes_accessed=tiles.size * 2 + source.size * 2 + out_blocks * out_rows * width * 2),
    )(*args)


def dense_kernel(recv_ref, w_ref, cot_ref, out_ref, pay_ref):
    agg = recv_ref[...].astype(jnp.float32).sum(0).astype(jnp.bfloat16)
    weight = w_ref[...]
    pre = jnp.dot(agg, weight, preferred_element_type=jnp.float32)
    sigma = jax.nn.sigmoid(pre)
    out_ref[...] = (pre * sigma).astype(out_ref.dtype)
    slope = sigma * (1.0 + pre * (1.0 - sigma))
    grad_pre = (cot_ref[...].astype(jnp.float32) * slope).astype(jnp.bfloat16)
    local_grad = lax.dot_general(agg, grad_pre, (((0,), (0,)), ((), ())),
                                 preferred_element_type=jnp.float32)
    grad_agg = lax.dot_general(grad_pre, weight, (((1,), (1,)), ((), ())),
                               preferred_element_type=jnp.float32).astype(pay_ref.dtype)
    tb = grad_agg.shape[0]
    blocks = pay_ref.shape[0]
    rows = local_grad.shape[0] // blocks
    half = local_grad.shape[1] // 2
    for j in range(blocks):
        pay_ref[j, :tb, :] = grad_agg
        part = local_grad[j * rows:(j + 1) * rows, :].astype(pay_ref.dtype)
        pay_ref[j, tb:tb + rows, :] = part[:, :half]
        pay_ref[j, tb + rows:tb + 2 * rows, :] = part[:, half:]


def dense(recv, weight, cot):
    blocks, tb, width_in = recv.shape
    width_out = weight.shape[1]
    rows = width_in // blocks
    vmem = pl.BlockSpec(memory_space=pltpu.VMEM)
    return pl.pallas_call(
        dense_kernel,
        out_shape=(
            jax.ShapeDtypeStruct((tb, width_out), jnp.bfloat16),
            jax.ShapeDtypeStruct((blocks, tb + 2 * rows, width_in), jnp.bfloat16),
        ),
        in_specs=[vmem, vmem, vmem],
        out_specs=(vmem, vmem),
        cost_estimate=pl.CostEstimate(
            flops=6 * tb * width_in * width_out, transcendentals=tb * width_out,
            bytes_accessed=recv.size * 2 + weight.size * 2 + cot.size * 2 + tb * width_out * 2
            + blocks * (tb + 2 * rows) * width_in * 2),
    )(*(pltpu.with_memory_space_constraint(x, pltpu.VMEM) for x in (recv, weight, cot)))


def on_device(features, weight, tile_values, tile_rows, tile_cols, tile_count, cotangent):
    rows_dev = features.shape[1]
    width_in = features.shape[2]
    width_out = weight.shape[1]
    tile_size = tile_values.shape[-1]
    n_row = lax.axis_size("row")
    n_col = lax.axis_size("col")
    row_tiles = rows_dev * n_col // tile_size
    col_tiles = rows_dev * n_row // tile_size
    node_total = rows_dev * n_row * n_col
    tile_block = tile_values[0, 0]
    row_ids = tile_rows[0, 0]
    col_ids = tile_cols[0, 0]
    tile_total = tile_count[0, 0]

    own = features[0]
    gathered = lax.all_to_all(
        jnp.broadcast_to(own[None], (n_row,) + own.shape), "row", 0, 0, tiled=False
    )
    col_source = gathered.reshape(col_tiles, tile_size, width_in)
    partial_value = spread(tile_block, row_ids, col_ids, tile_total, col_source, row_tiles, False, jnp.bfloat16)
    sent = partial_value.reshape(n_col, rows_dev, width_in)
    got = lax.all_to_all(sent, "col", 0, 0, tiled=False)
    out_block, payload = dense(got, weight, cotangent[0])
    output = out_block[None]
    wg_rows = width_in // n_col
    got = lax.all_to_all(payload, "col", 0, 0, tiled=False)
    row_source = got

    payload = spread(
        tile_block, col_ids, row_ids, tile_total, row_source, col_tiles, True, jnp.bfloat16, True
    )
    got = lax.all_to_all(payload, "row", 0, 0, tiled=False)
    grad_features = got[:, :rows_dev].astype(jnp.float32).sum(0).astype(jnp.bfloat16)[None]
    wg_part = got[:, rows_dev:].astype(jnp.float32).sum(0) * node_total ** (-0.5)
    wg_part = wg_part.reshape(2, wg_rows, width_in).transpose(1, 0, 2).reshape(wg_rows, width_out)

    everyone = lax.all_to_all(
        jnp.broadcast_to(wg_part[None], (n_col,) + wg_part.shape), "col", 0, 0, tiled=False
    )
    weight_grad = everyone.reshape(width_in, width_out)
    return (output, grad_features, weight_grad)


def solution(mesh):
    placed = (
        P("col", "row", None),
        P(),
        P("row", "col", None, None, None),
        P("row", "col", None),
        P("row", "col", None),
        P("row", "col"),
        P("row", "col", None),
    )
    return jax.shard_map(
        on_device,
        mesh=mesh,
        in_specs=placed,
        out_specs=(P("row", "col", None), P("col", "row", None), P()),
        check_vma=False,
    )
```

```python
import functools

import jax
import jax.numpy as jnp
from jax import lax
from jax.experimental import pallas as pl
from jax.experimental.pallas import tpu as pltpu
from jax.sharding import PartitionSpec as P


def spread_kernel(transpose, carry_words, rows_ref, cols_ref, count_ref, tiles_ref, src_ref, out_ref, acc_ref):
    tb = tiles_ref.shape[1]
    acc_ref[...] = jnp.zeros_like(acc_ref)
    live = count_ref[0]
    n_src = src_ref.shape[0] - 1
    n_acc = acc_ref.shape[0] - 1
    slots = tiles_ref.shape[0]
    group = 2 if slots % 2 == 0 else 1
    for first in range(0, slots, group):
        terms = []
        for t in range(first, first + group):
            tile = tiles_ref[t]
            src = src_ref[jnp.clip(cols_ref[t], 0, n_src), :tb, :]
            if transpose:
                term = lax.dot_general(tile, src, (((0,), (0,)), ((), ())),
                                       preferred_element_type=jnp.float32)
            else:
                term = jnp.dot(tile, src, preferred_element_type=jnp.float32)
            terms.append(jnp.where(t < live, term, 0.0))
        for t, term in zip(range(first, first + group), terms):
            acc_ref[jnp.clip(rows_ref[t], 0, n_acc)] += term
    if not carry_words:
        out_ref[...] = acc_ref[...].astype(out_ref.dtype)
    else:
        out_ref[:, :tb, :] = acc_ref[...].astype(out_ref.dtype)
        wg = jnp.zeros((src_ref.shape[1] - tb, src_ref.shape[2]), jnp.float32)
        for j in range(src_ref.shape[0]):
            wg = wg + src_ref[j, tb:, :].astype(jnp.float32)
        words = wg.astype(out_ref.dtype)
        for j in range(out_ref.shape[0]):
            out_ref[j, tb:, :] = words


def spread(tiles, target_ids, source_ids, count, source, out_blocks, transpose, out_dtype, carry_words=False):
    slots, tb, _ = tiles.shape
    width = source.shape[-1]
    smem = pl.BlockSpec(memory_space=pltpu.SMEM)
    vmem = pl.BlockSpec(memory_space=pltpu.VMEM)
    tiles = pltpu.with_memory_space_constraint(tiles, pltpu.VMEM)
    source = pltpu.with_memory_space_constraint(source, pltpu.VMEM)
    args = [target_ids, source_ids, count.reshape(1), tiles, source]
    out_rows = source.shape[1] if carry_words else tb
    return pl.pallas_call(
        functools.partial(spread_kernel, transpose, carry_words),
        out_shape=jax.ShapeDtypeStruct((out_blocks, out_rows, width), out_dtype),
        in_specs=[smem, smem, smem] + [vmem] * (len(args) - 3),
        out_specs=vmem,
        scratch_shapes=[pltpu.VMEM((out_blocks, tb, width), jnp.float32)],
        cost_estimate=pl.CostEstimate(
            flops=2 * slots * tb * tb * width, transcendentals=0,
            bytes_accessed=tiles.size * 2 + source.size * 2 + out_blocks * out_rows * width * 2),
    )(*args)


def dense_kernel(recv_ref, w_ref, cot_ref, out_ref, pay_ref):
    agg = recv_ref[...].astype(jnp.float32).sum(0).astype(jnp.bfloat16)
    weight = w_ref[...]
    pre = jnp.dot(agg, weight, preferred_element_type=jnp.float32)
    sigma = jax.nn.sigmoid(pre)
    out_ref[...] = (pre * sigma).astype(out_ref.dtype)
    slope = sigma * (1.0 + pre * (1.0 - sigma))
    grad_pre = (cot_ref[...].astype(jnp.float32) * slope).astype(jnp.bfloat16)
    local_grad = lax.dot_general(agg, grad_pre, (((0,), (0,)), ((), ())),
                                 preferred_element_type=jnp.float32)
    grad_agg = lax.dot_general(grad_pre, weight, (((1,), (1,)), ((), ())),
                               preferred_element_type=jnp.float32).astype(pay_ref.dtype)
    tb = grad_agg.shape[0]
    blocks = pay_ref.shape[0]
    rows = local_grad.shape[0] // blocks
    half = local_grad.shape[1] // 2
    for j in range(blocks):
        pay_ref[j, :tb, :] = grad_agg
        part = local_grad[j * rows:(j + 1) * rows, :].astype(pay_ref.dtype)
        pay_ref[j, tb:tb + rows, :] = part[:, :half]
        pay_ref[j, tb + rows:tb + 2 * rows, :] = part[:, half:]


def dense(recv, weight, cot):
    blocks, tb, width_in = recv.shape
    width_out = weight.shape[1]
    rows = width_in // blocks
    vmem = pl.BlockSpec(memory_space=pltpu.VMEM)
    return pl.pallas_call(
        dense_kernel,
        out_shape=(
            jax.ShapeDtypeStruct((tb, width_out), jnp.bfloat16),
            jax.ShapeDtypeStruct((blocks, tb + 2 * rows, width_in), jnp.bfloat16),
        ),
        in_specs=[vmem, vmem, vmem],
        out_specs=(vmem, vmem),
        cost_estimate=pl.CostEstimate(
            flops=6 * tb * width_in * width_out, transcendentals=tb * width_out,
            bytes_accessed=recv.size * 2 + weight.size * 2 + cot.size * 2 + tb * width_out * 2
            + blocks * (tb + 2 * rows) * width_in * 2),
    )(*(pltpu.with_memory_space_constraint(x, pltpu.VMEM) for x in (recv, weight, cot)))


def weight_part_kernel(tb, rows, scale, got_ref, out_ref):
    wg = jnp.zeros((2 * rows, got_ref.shape[2]), jnp.float32)
    for j in range(got_ref.shape[0]):
        wg = wg + got_ref[j, tb:, :].astype(jnp.float32)
    wg = wg * scale
    half = got_ref.shape[2]
    for j in range(out_ref.shape[0]):
        out_ref[j, :, :half] = wg[:rows]
        out_ref[j, :, half:] = wg[rows:]


def weight_part(got, tb, rows, copies, scale):
    width = got.shape[2]
    vmem = pl.BlockSpec(memory_space=pltpu.VMEM)
    return pl.pallas_call(
        functools.partial(weight_part_kernel, tb, rows, scale),
        out_shape=jax.ShapeDtypeStruct((copies, rows, 2 * width), jnp.float32),
        in_specs=[vmem],
        out_specs=vmem,
        cost_estimate=pl.CostEstimate(
            flops=got.shape[0] * 2 * rows * width, transcendentals=0,
            bytes_accessed=got.shape[0] * 2 * rows * width * 2 + copies * rows * 2 * width * 4),
    )(pltpu.with_memory_space_constraint(got, pltpu.VMEM))


def on_device(features, weight, tile_values, tile_rows, tile_cols, tile_count, cotangent):
    rows_dev = features.shape[1]
    width_in = features.shape[2]
    width_out = weight.shape[1]
    tile_size = tile_values.shape[-1]
    n_row = lax.axis_size("row")
    n_col = lax.axis_size("col")
    row_tiles = rows_dev * n_col // tile_size
    col_tiles = rows_dev * n_row // tile_size
    node_total = rows_dev * n_row * n_col
    tile_block = tile_values[0, 0]
    row_ids = tile_rows[0, 0]
    col_ids = tile_cols[0, 0]
    tile_total = tile_count[0, 0]

    own = features[0]
    gathered = lax.all_to_all(
        jnp.broadcast_to(own[None], (n_row,) + own.shape), "row", 0, 0, tiled=False
    )
    col_source = gathered.reshape(col_tiles, tile_size, width_in)
    partial_value = spread(tile_block, row_ids, col_ids, tile_total, col_source, row_tiles, False, jnp.bfloat16)
    sent = partial_value.reshape(n_col, rows_dev, width_in)
    got = lax.all_to_all(sent, "col", 0, 0, tiled=False)
    out_block, payload = dense(got, weight, cotangent[0])
    output = out_block[None]
    wg_rows = width_in // n_col
    got = lax.all_to_all(payload, "col", 0, 0, tiled=False)
    row_source = got

    payload = spread(
        tile_block, col_ids, row_ids, tile_total, row_source, col_tiles, True, jnp.bfloat16, True
    )
    got = lax.all_to_all(payload, "row", 0, 0, tiled=False)
    grad_features = got[:, :rows_dev].astype(jnp.float32).sum(0).astype(jnp.bfloat16)[None]
    parts = weight_part(got, rows_dev, wg_rows, n_col, node_total ** (-0.5))

    everyone = lax.all_to_all(parts, "col", 0, 0, tiled=False)
    weight_grad = everyone.reshape(width_in, width_out)
    return (output, grad_features, weight_grad)


def solution(mesh):
    placed = (
        P("col", "row", None),
        P(),
        P("row", "col", None, None, None),
        P("row", "col", None),
        P("row", "col", None),
        P("row", "col"),
        P("row", "col", None),
    )
    return jax.shard_map(
        on_device,
        mesh=mesh,
        in_specs=placed,
        out_specs=(P("row", "col", None), P("col", "row", None), P()),
        check_vma=False,
    )
```

```python
import functools

import jax
import jax.numpy as jnp
from jax import lax
from jax.experimental import pallas as pl
from jax.experimental.pallas import tpu as pltpu
from jax.sharding import PartitionSpec as P


def spread_kernel(transpose, carry_words, rows_ref, cols_ref, count_ref, tiles_ref, src_ref, out_ref, acc_ref):
    tb = tiles_ref.shape[1]
    acc_ref[...] = jnp.zeros_like(acc_ref)
    live = count_ref[0]
    n_src = src_ref.shape[0] - 1
    n_acc = acc_ref.shape[0] - 1
    slots = tiles_ref.shape[0]
    group = 2 if slots % 2 == 0 else 1
    for first in range(0, slots, group):
        terms = []
        for t in range(first, first + group):
            tile = jnp.where(t < live, tiles_ref[t], jnp.zeros((), tiles_ref.dtype))
            src = src_ref[jnp.clip(cols_ref[t], 0, n_src), :tb, :]
            if transpose:
                term = lax.dot_general(tile, src, (((0,), (0,)), ((), ())),
                                       preferred_element_type=jnp.float32)
            else:
                term = jnp.dot(tile, src, preferred_element_type=jnp.float32)
            terms.append(term)
        for t, term in zip(range(first, first + group), terms):
            acc_ref[jnp.clip(rows_ref[t], 0, n_acc)] += term
    if not carry_words:
        out_ref[...] = acc_ref[...].astype(out_ref.dtype)
    else:
        out_ref[:, :tb, :] = acc_ref[...].astype(out_ref.dtype)
        wg = jnp.zeros((src_ref.shape[1] - tb, src_ref.shape[2]), jnp.float32)
        for j in range(src_ref.shape[0]):
            wg = wg + src_ref[j, tb:, :].astype(jnp.float32)
        words = wg.astype(out_ref.dtype)
        for j in range(out_ref.shape[0]):
            out_ref[j, tb:, :] = words


def spread(tiles, target_ids, source_ids, count, source, out_blocks, transpose, out_dtype, carry_words=False):
    slots, tb, _ = tiles.shape
    width = source.shape[-1]
    smem = pl.BlockSpec(memory_space=pltpu.SMEM)
    vmem = pl.BlockSpec(memory_space=pltpu.VMEM)
    tiles = pltpu.with_memory_space_constraint(tiles, pltpu.VMEM)
    source = pltpu.with_memory_space_constraint(source, pltpu.VMEM)
    args = [target_ids, source_ids, count.reshape(1), tiles, source]
    out_rows = source.shape[1] if carry_words else tb
    return pl.pallas_call(
        functools.partial(spread_kernel, transpose, carry_words),
        out_shape=jax.ShapeDtypeStruct((out_blocks, out_rows, width), out_dtype),
        in_specs=[smem, smem, smem] + [vmem] * (len(args) - 3),
        out_specs=vmem,
        scratch_shapes=[pltpu.VMEM((out_blocks, tb, width), jnp.float32)],
        cost_estimate=pl.CostEstimate(
            flops=2 * slots * tb * tb * width, transcendentals=0,
            bytes_accessed=tiles.size * 2 + source.size * 2 + out_blocks * out_rows * width * 2),
    )(*args)


def dense_kernel(recv_ref, w_ref, cot_ref, out_ref, pay_ref):
    agg = recv_ref[...].astype(jnp.float32).sum(0).astype(jnp.bfloat16)
    weight = w_ref[...]
    pre = jnp.dot(agg, weight, preferred_element_type=jnp.float32)
    sigma = jax.nn.sigmoid(pre)
    out_ref[...] = (pre * sigma).astype(out_ref.dtype)
    slope = sigma * (1.0 + pre * (1.0 - sigma))
    grad_pre = (cot_ref[...].astype(jnp.float32) * slope).astype(jnp.bfloat16)
    local_grad = lax.dot_general(agg, grad_pre, (((0,), (0,)), ((), ())),
                                 preferred_element_type=jnp.float32)
    grad_agg = lax.dot_general(grad_pre, weight, (((1,), (1,)), ((), ())),
                               preferred_element_type=jnp.float32).astype(pay_ref.dtype)
    tb = grad_agg.shape[0]
    blocks = pay_ref.shape[0]
    rows = local_grad.shape[0] // blocks
    half = local_grad.shape[1] // 2
    for j in range(blocks):
        pay_ref[j, :tb, :] = grad_agg
        part = local_grad[j * rows:(j + 1) * rows, :].astype(pay_ref.dtype)
        pay_ref[j, tb:tb + rows, :] = part[:, :half]
        pay_ref[j, tb + rows:tb + 2 * rows, :] = part[:, half:]


def dense(recv, weight, cot):
    blocks, tb, width_in = recv.shape
    width_out = weight.shape[1]
    rows = width_in // blocks
    vmem = pl.BlockSpec(memory_space=pltpu.VMEM)
    return pl.pallas_call(
        dense_kernel,
        out_shape=(
            jax.ShapeDtypeStruct((tb, width_out), jnp.bfloat16),
            jax.ShapeDtypeStruct((blocks, tb + 2 * rows, width_in), jnp.bfloat16),
        ),
        in_specs=[vmem, vmem, vmem],
        out_specs=(vmem, vmem),
        cost_estimate=pl.CostEstimate(
            flops=6 * tb * width_in * width_out, transcendentals=tb * width_out,
            bytes_accessed=recv.size * 2 + weight.size * 2 + cot.size * 2 + tb * width_out * 2
            + blocks * (tb + 2 * rows) * width_in * 2),
    )(*(pltpu.with_memory_space_constraint(x, pltpu.VMEM) for x in (recv, weight, cot)))


def on_device(features, weight, tile_values, tile_rows, tile_cols, tile_count, cotangent):
    rows_dev = features.shape[1]
    width_in = features.shape[2]
    width_out = weight.shape[1]
    tile_size = tile_values.shape[-1]
    n_row = lax.axis_size("row")
    n_col = lax.axis_size("col")
    row_tiles = rows_dev * n_col // tile_size
    col_tiles = rows_dev * n_row // tile_size
    node_total = rows_dev * n_row * n_col
    tile_block = tile_values[0, 0]
    row_ids = tile_rows[0, 0]
    col_ids = tile_cols[0, 0]
    tile_total = tile_count[0, 0]

    own = features[0]
    gathered = lax.all_to_all(
        jnp.broadcast_to(own[None], (n_row,) + own.shape), "row", 0, 0, tiled=False
    )
    col_source = gathered.reshape(col_tiles, tile_size, width_in)
    partial_value = spread(tile_block, row_ids, col_ids, tile_total, col_source, row_tiles, False, jnp.bfloat16)
    sent = partial_value.reshape(n_col, rows_dev, width_in)
    got = lax.all_to_all(sent, "col", 0, 0, tiled=False)
    out_block, payload = dense(got, weight, cotangent[0])
    output = out_block[None]
    wg_rows = width_in // n_col
    got = lax.all_to_all(payload, "col", 0, 0, tiled=False)
    row_source = got

    payload = spread(
        tile_block, col_ids, row_ids, tile_total, row_source, col_tiles, True, jnp.bfloat16, True
    )
    got = lax.all_to_all(payload, "row", 0, 0, tiled=False)
    grad_features = got[:, :rows_dev].astype(jnp.float32).sum(0).astype(jnp.bfloat16)[None]
    wg_part = got[:, rows_dev:].astype(jnp.float32).sum(0) * node_total ** (-0.5)
    wg_part = wg_part.reshape(2, wg_rows, width_in).transpose(1, 0, 2).reshape(wg_rows, width_out)

    everyone = lax.all_to_all(
        jnp.broadcast_to(wg_part[None], (n_col,) + wg_part.shape), "col", 0, 0, tiled=False
    )
    weight_grad = everyone.reshape(width_in, width_out)
    return (output, grad_features, weight_grad)


def solution(mesh):
    placed = (
        P("col", "row", None),
        P(),
        P("row", "col", None, None, None),
        P("row", "col", None),
        P("row", "col", None),
        P("row", "col"),
        P("row", "col", None),
    )
    return jax.shard_map(
        on_device,
        mesh=mesh,
        in_specs=placed,
        out_specs=(P("row", "col", None), P("col", "row", None), P()),
        check_vma=False,
    )
```

```python
import functools

import jax
import jax.numpy as jnp
from jax import lax
from jax.experimental import pallas as pl
from jax.experimental.pallas import tpu as pltpu
from jax.sharding import PartitionSpec as P


def spread_kernel(transpose, carry_words, rows_ref, cols_ref, count_ref, tiles_ref, src_ref, out_ref, acc_ref):
    tb = tiles_ref.shape[1]
    acc_ref[...] = jnp.zeros_like(acc_ref)
    live = count_ref[0]
    n_src = src_ref.shape[0] - 1
    n_acc = acc_ref.shape[0] - 1
    slots = tiles_ref.shape[0]
    group = 2 if slots % 2 == 0 else 1
    for first in range(0, slots, group):
        terms = []
        for t in range(first, first + group):
            tile = tiles_ref[t]
            src = src_ref[jnp.clip(cols_ref[t], 0, n_src), :tb, :]
            if transpose:
                term = lax.dot_general(tile, src, (((0,), (0,)), ((), ())),
                                       preferred_element_type=jnp.float32)
            else:
                term = jnp.dot(tile, src, preferred_element_type=jnp.float32)
            terms.append(jnp.where(t < live, term, 0.0))
        for t, term in zip(range(first, first + group), terms):
            acc_ref[jnp.clip(rows_ref[t], 0, n_acc)] += term
    if not carry_words:
        out_ref[...] = acc_ref[...].astype(out_ref.dtype)
    else:
        out_ref[:, :tb, :] = acc_ref[...].astype(out_ref.dtype)
        wg = jnp.zeros((src_ref.shape[1] - tb, src_ref.shape[2]), jnp.float32)
        for j in range(src_ref.shape[0]):
            wg = wg + src_ref[j, tb:, :].astype(jnp.float32)
        words = wg.astype(out_ref.dtype)
        for j in range(out_ref.shape[0]):
            out_ref[j, tb:, :] = words


def spread(tiles, target_ids, source_ids, count, source, out_blocks, transpose, out_dtype, carry_words=False):
    slots, tb, _ = tiles.shape
    width = source.shape[-1]
    smem = pl.BlockSpec(memory_space=pltpu.SMEM)
    vmem = pl.BlockSpec(memory_space=pltpu.VMEM)
    tiles = pltpu.with_memory_space_constraint(tiles, pltpu.VMEM)
    source = pltpu.with_memory_space_constraint(source, pltpu.VMEM)
    args = [target_ids, source_ids, count.reshape(1), tiles, source]
    out_rows = source.shape[1] if carry_words else tb
    return pl.pallas_call(
        functools.partial(spread_kernel, transpose, carry_words),
        out_shape=jax.ShapeDtypeStruct((out_blocks, out_rows, width), out_dtype),
        in_specs=[smem, smem, smem] + [vmem] * (len(args) - 3),
        out_specs=vmem,
        scratch_shapes=[pltpu.VMEM((out_blocks, tb, width), jnp.float32)],
        cost_estimate=pl.CostEstimate(
            flops=2 * slots * tb * tb * width, transcendentals=0,
            bytes_accessed=tiles.size * 2 + source.size * 2 + out_blocks * out_rows * width * 2),
    )(*args)


def dense_kernel(recv_ref, w_ref, cot_ref, out_ref, pay_ref):
    agg = recv_ref[...].astype(jnp.float32).sum(0).astype(jnp.bfloat16)
    weight = w_ref[...]
    pre = jnp.dot(agg, weight, preferred_element_type=jnp.float32)
    sigma = jax.nn.sigmoid(pre)
    out_ref[...] = (pre * sigma).astype(out_ref.dtype)
    slope = sigma * (1.0 + pre * (1.0 - sigma))
    grad_pre = (cot_ref[...].astype(jnp.float32) * slope).astype(jnp.bfloat16)
    local_grad = lax.dot_general(agg, grad_pre, (((0,), (0,)), ((), ())),
                                 preferred_element_type=jnp.float32)
    grad_agg = lax.dot_general(grad_pre, weight, (((1,), (1,)), ((), ())),
                               preferred_element_type=jnp.float32).astype(pay_ref.dtype)
    tb = grad_agg.shape[0]
    blocks = pay_ref.shape[0]
    rows = local_grad.shape[0] // blocks
    half = local_grad.shape[1] // 2
    for j in range(blocks):
        pay_ref[j, :tb, :] = grad_agg
        part = local_grad[j * rows:(j + 1) * rows, :].astype(pay_ref.dtype)
        pay_ref[j, tb:tb + rows, :] = part[:, :half]
        pay_ref[j, tb + rows:tb + 2 * rows, :] = part[:, half:]


def dense(recv, weight, cot):
    blocks, tb, width_in = recv.shape
    width_out = weight.shape[1]
    rows = width_in // blocks
    vmem = pl.BlockSpec(memory_space=pltpu.VMEM)
    return pl.pallas_call(
        dense_kernel,
        out_shape=(
            jax.ShapeDtypeStruct((tb, width_out), jnp.bfloat16),
            jax.ShapeDtypeStruct((blocks, tb + 2 * rows, width_in), jnp.bfloat16),
        ),
        in_specs=[vmem, vmem, vmem],
        out_specs=(vmem, vmem),
        cost_estimate=pl.CostEstimate(
            flops=6 * tb * width_in * width_out, transcendentals=tb * width_out,
            bytes_accessed=recv.size * 2 + weight.size * 2 + cot.size * 2 + tb * width_out * 2
            + blocks * (tb + 2 * rows) * width_in * 2),
    )(*(pltpu.with_memory_space_constraint(x, pltpu.VMEM) for x in (recv, weight, cot)))


def replicate_kernel(x_ref, out_ref):
    out_ref[...] = jnp.broadcast_to(x_ref[...], out_ref.shape)


def replicate(x, copies):
    vmem = pl.BlockSpec(memory_space=pltpu.VMEM)
    return pl.pallas_call(
        replicate_kernel,
        out_shape=jax.ShapeDtypeStruct((copies,) + x.shape[1:], x.dtype),
        in_specs=[vmem],
        out_specs=vmem,
        cost_estimate=pl.CostEstimate(
            flops=0, transcendentals=0, bytes_accessed=(copies + 1) * x.size * x.dtype.itemsize),
    )(pltpu.with_memory_space_constraint(x, pltpu.VMEM))


def on_device(features, weight, tile_values, tile_rows, tile_cols, tile_count, cotangent):
    rows_dev = features.shape[1]
    width_in = features.shape[2]
    width_out = weight.shape[1]
    tile_size = tile_values.shape[-1]
    n_row = lax.axis_size("row")
    n_col = lax.axis_size("col")
    row_tiles = rows_dev * n_col // tile_size
    col_tiles = rows_dev * n_row // tile_size
    node_total = rows_dev * n_row * n_col
    tile_block = tile_values[0, 0]
    row_ids = tile_rows[0, 0]
    col_ids = tile_cols[0, 0]
    tile_total = tile_count[0, 0]

    gathered = lax.all_to_all(replicate(features, n_row), "row", 0, 0, tiled=False)
    col_source = gathered.reshape(col_tiles, tile_size, width_in)
    partial_value = spread(tile_block, row_ids, col_ids, tile_total, col_source, row_tiles, False, jnp.bfloat16)
    sent = partial_value.reshape(n_col, rows_dev, width_in)
    got = lax.all_to_all(sent, "col", 0, 0, tiled=False)
    out_block, payload = dense(got, weight, cotangent[0])
    output = out_block[None]
    wg_rows = width_in // n_col
    got = lax.all_to_all(payload, "col", 0, 0, tiled=False)
    row_source = got

    payload = spread(
        tile_block, col_ids, row_ids, tile_total, row_source, col_tiles, True, jnp.bfloat16, True
    )
    got = lax.all_to_all(payload, "row", 0, 0, tiled=False)
    grad_features = got[:, :rows_dev].astype(jnp.float32).sum(0).astype(jnp.bfloat16)[None]
    wg_part = got[:, rows_dev:].astype(jnp.float32).sum(0) * node_total ** (-0.5)
    wg_part = wg_part.reshape(2, wg_rows, width_in).transpose(1, 0, 2).reshape(wg_rows, width_out)

    everyone = lax.all_to_all(
        jnp.broadcast_to(wg_part[None], (n_col,) + wg_part.shape), "col", 0, 0, tiled=False
    )
    weight_grad = everyone.reshape(width_in, width_out)
    return (output, grad_features, weight_grad)


def solution(mesh):
    placed = (
        P("col", "row", None),
        P(),
        P("row", "col", None, None, None),
        P("row", "col", None),
        P("row", "col", None),
        P("row", "col"),
        P("row", "col", None),
    )
    return jax.shard_map(
        on_device,
        mesh=mesh,
        in_specs=placed,
        out_specs=(P("row", "col", None), P("col", "row", None), P()),
        check_vma=False,
    )
```

```python
import functools

import jax
import jax.numpy as jnp
from jax import lax
from jax.experimental import pallas as pl
from jax.experimental.pallas import tpu as pltpu
from jax.sharding import PartitionSpec as P


def spread_kernel(transpose, carry_words, rows_ref, cols_ref, count_ref, tiles_ref, src_ref, out_ref, acc_ref):
    tb = tiles_ref.shape[1]
    acc_ref[...] = jnp.zeros_like(acc_ref)
    live = count_ref[0]
    n_src = src_ref.shape[0] - 1
    n_acc = acc_ref.shape[0] - 1
    slots = tiles_ref.shape[0]
    group = 4 if slots % 4 == 0 else 1
    for first in range(0, slots, group):
        terms = []
        for t in range(first, first + group):
            tile = tiles_ref[t]
            src = src_ref[jnp.clip(cols_ref[t], 0, n_src), :tb, :]
            if transpose:
                term = lax.dot_general(tile, src, (((0,), (0,)), ((), ())),
                                       preferred_element_type=jnp.float32)
            else:
                term = jnp.dot(tile, src, preferred_element_type=jnp.float32)
            terms.append(jnp.where(t < live, term, 0.0))
        for t, term in zip(range(first, first + group), terms):
            acc_ref[jnp.clip(rows_ref[t], 0, n_acc)] += term
    if not carry_words:
        out_ref[...] = acc_ref[...].astype(out_ref.dtype)
    else:
        out_ref[:, :tb, :] = acc_ref[...].astype(out_ref.dtype)
        wg = jnp.zeros((src_ref.shape[1] - tb, src_ref.shape[2]), jnp.float32)
        for j in range(src_ref.shape[0]):
            wg = wg + src_ref[j, tb:, :].astype(jnp.float32)
        words = wg.astype(out_ref.dtype)
        for j in range(out_ref.shape[0]):
            out_ref[j, tb:, :] = words


def spread(tiles, target_ids, source_ids, count, source, out_blocks, transpose, out_dtype, carry_words=False):
    slots, tb, _ = tiles.shape
    width = source.shape[-1]
    smem = pl.BlockSpec(memory_space=pltpu.SMEM)
    vmem = pl.BlockSpec(memory_space=pltpu.VMEM)
    tiles = pltpu.with_memory_space_constraint(tiles, pltpu.VMEM)
    source = pltpu.with_memory_space_constraint(source, pltpu.VMEM)
    args = [target_ids, source_ids, count.reshape(1), tiles, source]
    out_rows = source.shape[1] if carry_words else tb
    return pl.pallas_call(
        functools.partial(spread_kernel, transpose, carry_words),
        out_shape=jax.ShapeDtypeStruct((out_blocks, out_rows, width), out_dtype),
        in_specs=[smem, smem, smem] + [vmem] * (len(args) - 3),
        out_specs=vmem,
        scratch_shapes=[pltpu.VMEM((out_blocks, tb, width), jnp.float32)],
        cost_estimate=pl.CostEstimate(
            flops=2 * slots * tb * tb * width, transcendentals=0,
            bytes_accessed=tiles.size * 2 + source.size * 2 + out_blocks * out_rows * width * 2),
    )(*args)


def dense_kernel(recv_ref, w_ref, cot_ref, out_ref, pay_ref):
    agg = recv_ref[...].astype(jnp.float32).sum(0).astype(jnp.bfloat16)
    weight = w_ref[...]
    pre = jnp.dot(agg, weight, preferred_element_type=jnp.float32)
    sigma = jax.nn.sigmoid(pre)
    out_ref[...] = (pre * sigma).astype(out_ref.dtype)
    slope = sigma * (1.0 + pre * (1.0 - sigma))
    grad_pre = (cot_ref[...].astype(jnp.float32) * slope).astype(jnp.bfloat16)
    local_grad = lax.dot_general(agg, grad_pre, (((0,), (0,)), ((), ())),
                                 preferred_element_type=jnp.float32)
    grad_agg = lax.dot_general(grad_pre, weight, (((1,), (1,)), ((), ())),
                               preferred_element_type=jnp.float32).astype(pay_ref.dtype)
    tb = grad_agg.shape[0]
    blocks = pay_ref.shape[0]
    rows = local_grad.shape[0] // blocks
    half = local_grad.shape[1] // 2
    for j in range(blocks):
        pay_ref[j, :tb, :] = grad_agg
        part = local_grad[j * rows:(j + 1) * rows, :].astype(pay_ref.dtype)
        pay_ref[j, tb:tb + rows, :] = part[:, :half]
        pay_ref[j, tb + rows:tb + 2 * rows, :] = part[:, half:]


def dense(recv, weight, cot):
    blocks, tb, width_in = recv.shape
    width_out = weight.shape[1]
    rows = width_in // blocks
    vmem = pl.BlockSpec(memory_space=pltpu.VMEM)
    return pl.pallas_call(
        dense_kernel,
        out_shape=(
            jax.ShapeDtypeStruct((tb, width_out), jnp.bfloat16),
            jax.ShapeDtypeStruct((blocks, tb + 2 * rows, width_in), jnp.bfloat16),
        ),
        in_specs=[vmem, vmem, vmem],
        out_specs=(vmem, vmem),
        cost_estimate=pl.CostEstimate(
            flops=6 * tb * width_in * width_out, transcendentals=tb * width_out,
            bytes_accessed=recv.size * 2 + weight.size * 2 + cot.size * 2 + tb * width_out * 2
            + blocks * (tb + 2 * rows) * width_in * 2),
    )(*(pltpu.with_memory_space_constraint(x, pltpu.VMEM) for x in (recv, weight, cot)))


def replicate_kernel(x_ref, out_ref):
    out_ref[...] = jnp.broadcast_to(x_ref[...], out_ref.shape)


def replicate(x, copies):
    vmem = pl.BlockSpec(memory_space=pltpu.VMEM)
    return pl.pallas_call(
        replicate_kernel,
        out_shape=jax.ShapeDtypeStruct((copies,) + x.shape[1:], x.dtype),
        in_specs=[vmem],
        out_specs=vmem,
        cost_estimate=pl.CostEstimate(
            flops=0, transcendentals=0, bytes_accessed=(copies + 1) * x.size * x.dtype.itemsize),
    )(pltpu.with_memory_space_constraint(x, pltpu.VMEM))


def on_device(features, weight, tile_values, tile_rows, tile_cols, tile_count, cotangent):
    rows_dev = features.shape[1]
    width_in = features.shape[2]
    width_out = weight.shape[1]
    tile_size = tile_values.shape[-1]
    n_row = lax.axis_size("row")
    n_col = lax.axis_size("col")
    row_tiles = rows_dev * n_col // tile_size
    col_tiles = rows_dev * n_row // tile_size
    node_total = rows_dev * n_row * n_col
    tile_block = tile_values[0, 0]
    row_ids = tile_rows[0, 0]
    col_ids = tile_cols[0, 0]
    tile_total = tile_count[0, 0]

    gathered = lax.all_to_all(replicate(features, n_row), "row", 0, 0, tiled=False)
    col_source = gathered.reshape(col_tiles, tile_size, width_in)
    partial_value = spread(tile_block, row_ids, col_ids, tile_total, col_source, row_tiles, False, jnp.bfloat16)
    sent = partial_value.reshape(n_col, rows_dev, width_in)
    got = lax.all_to_all(sent, "col", 0, 0, tiled=False)
    out_block, payload = dense(got, weight, cotangent[0])
    output = out_block[None]
    wg_rows = width_in // n_col
    got = lax.all_to_all(payload, "col", 0, 0, tiled=False)
    row_source = got

    payload = spread(
        tile_block, col_ids, row_ids, tile_total, row_source, col_tiles, True, jnp.bfloat16, True
    )
    got = lax.all_to_all(payload, "row", 0, 0, tiled=False)
    grad_features = got[:, :rows_dev].astype(jnp.float32).sum(0).astype(jnp.bfloat16)[None]
    wg_part = got[:, rows_dev:].astype(jnp.float32).sum(0) * node_total ** (-0.5)
    wg_part = wg_part.reshape(2, wg_rows, width_in).transpose(1, 0, 2).reshape(wg_rows, width_out)

    everyone = lax.all_to_all(
        jnp.broadcast_to(wg_part[None], (n_col,) + wg_part.shape), "col", 0, 0, tiled=False
    )
    weight_grad = everyone.reshape(width_in, width_out)
    return (output, grad_features, weight_grad)


def solution(mesh):
    placed = (
        P("col", "row", None),
        P(),
        P("row", "col", None, None, None),
        P("row", "col", None),
        P("row", "col", None),
        P("row", "col"),
        P("row", "col", None),
    )
    return jax.shard_map(
        on_device,
        mesh=mesh,
        in_specs=placed,
        out_specs=(P("row", "col", None), P("col", "row", None), P()),
        check_vma=False,
    )
```

```python
import functools

import jax
import jax.numpy as jnp
from jax import lax
from jax.experimental import pallas as pl
from jax.experimental.pallas import tpu as pltpu
from jax.sharding import PartitionSpec as P


def spread_kernel(transpose, carry_words, rows_ref, cols_ref, count_ref, tiles_ref, src_ref, out_ref, acc_ref):
    tb = tiles_ref.shape[1]
    acc_ref[...] = jnp.zeros_like(acc_ref)
    live = count_ref[0]
    n_src = src_ref.shape[0] - 1
    n_acc = acc_ref.shape[0] - 1
    slots = tiles_ref.shape[0]
    group = 4 if slots % 4 == 0 else 1
    for first in range(0, slots, group):
        terms = []
        for t in range(first, first + group):
            tile = tiles_ref[t]
            src = src_ref[jnp.clip(cols_ref[t], 0, n_src), :tb, :]
            if transpose:
                term = lax.dot_general(tile, src, (((0,), (0,)), ((), ())),
                                       preferred_element_type=jnp.float32)
            else:
                term = jnp.dot(tile, src, preferred_element_type=jnp.float32)
            terms.append(jnp.where(t < live, term, 0.0))
        for t, term in zip(range(first, first + group), terms):
            acc_ref[jnp.clip(rows_ref[t], 0, n_acc)] += term
    if not carry_words:
        out_ref[...] = acc_ref[...].astype(out_ref.dtype)
    else:
        out_ref[:, :tb, :] = acc_ref[...].astype(out_ref.dtype)
        wg = jnp.zeros((src_ref.shape[1] - tb, src_ref.shape[2]), jnp.float32)
        for j in range(src_ref.shape[0]):
            wg = wg + src_ref[j, tb:, :].astype(jnp.float32)
        words = wg.astype(out_ref.dtype)
        for j in range(out_ref.shape[0]):
            out_ref[j, tb:, :] = words


def spread(tiles, target_ids, source_ids, count, source, out_blocks, transpose, out_dtype, carry_words=False):
    slots, tb, _ = tiles.shape
    width = source.shape[-1]
    smem = pl.BlockSpec(memory_space=pltpu.SMEM)
    vmem = pl.BlockSpec(memory_space=pltpu.VMEM)
    tiles = pltpu.with_memory_space_constraint(tiles, pltpu.VMEM)
    source = pltpu.with_memory_space_constraint(source, pltpu.VMEM)
    args = [target_ids, source_ids, count.reshape(1), tiles, source]
    out_rows = source.shape[1] if carry_words else tb
    return pl.pallas_call(
        functools.partial(spread_kernel, transpose, carry_words),
        out_shape=jax.ShapeDtypeStruct((out_blocks, out_rows, width), out_dtype),
        in_specs=[smem, smem, smem] + [vmem] * (len(args) - 3),
        out_specs=vmem,
        scratch_shapes=[pltpu.VMEM((out_blocks, tb, width), jnp.float32)],
        cost_estimate=pl.CostEstimate(
            flops=2 * slots * tb * tb * width, transcendentals=0,
            bytes_accessed=tiles.size * 2 + source.size * 2 + out_blocks * out_rows * width * 2),
    )(*args)


def dense_kernel(recv_ref, w_ref, cot_ref, out_ref, pay_ref):
    agg = recv_ref[...].astype(jnp.float32).sum(0).astype(jnp.bfloat16)
    weight = w_ref[...]
    pre = jnp.dot(agg, weight, preferred_element_type=jnp.float32)
    sigma = jax.nn.sigmoid(pre)
    out_ref[...] = (pre * sigma).astype(out_ref.dtype)
    slope = sigma * (1.0 + pre * (1.0 - sigma))
    grad_pre = (cot_ref[...].astype(jnp.float32) * slope).astype(jnp.bfloat16)
    local_grad = lax.dot_general(agg, grad_pre, (((0,), (0,)), ((), ())),
                                 preferred_element_type=jnp.float32)
    grad_agg = lax.dot_general(grad_pre, weight, (((1,), (1,)), ((), ())),
                               preferred_element_type=jnp.float32).astype(pay_ref.dtype)
    tb = grad_agg.shape[0]
    blocks = pay_ref.shape[0]
    rows = local_grad.shape[0] // blocks
    half = local_grad.shape[1] // 2
    for j in range(blocks):
        pay_ref[j, :tb, :] = grad_agg
        part = local_grad[j * rows:(j + 1) * rows, :].astype(pay_ref.dtype)
        pay_ref[j, tb:tb + rows, :] = part[:, :half]
        pay_ref[j, tb + rows:tb + 2 * rows, :] = part[:, half:]


def dense(recv, weight, cot):
    blocks, tb, width_in = recv.shape
    width_out = weight.shape[1]
    rows = width_in // blocks
    vmem = pl.BlockSpec(memory_space=pltpu.VMEM)
    return pl.pallas_call(
        dense_kernel,
        out_shape=(
            jax.ShapeDtypeStruct((tb, width_out), jnp.bfloat16),
            jax.ShapeDtypeStruct((blocks, tb + 2 * rows, width_in), jnp.bfloat16),
        ),
        in_specs=[vmem, vmem, vmem],
        out_specs=(vmem, vmem),
        cost_estimate=pl.CostEstimate(
            flops=6 * tb * width_in * width_out, transcendentals=tb * width_out,
            bytes_accessed=recv.size * 2 + weight.size * 2 + cot.size * 2 + tb * width_out * 2
            + blocks * (tb + 2 * rows) * width_in * 2),
    )(*(pltpu.with_memory_space_constraint(x, pltpu.VMEM) for x in (recv, weight, cot)))


def replicate_kernel(x_ref, out_ref):
    out_ref[...] = jnp.broadcast_to(x_ref[...], out_ref.shape)


def replicate(x, copies):
    vmem = pl.BlockSpec(memory_space=pltpu.VMEM)
    return pl.pallas_call(
        replicate_kernel,
        out_shape=jax.ShapeDtypeStruct((copies,) + x.shape[1:], x.dtype),
        in_specs=[vmem],
        out_specs=vmem,
        cost_estimate=pl.CostEstimate(
            flops=0, transcendentals=0, bytes_accessed=(copies + 1) * x.size * x.dtype.itemsize),
    )(pltpu.with_memory_space_constraint(x, pltpu.VMEM))


def weight_part_kernel(tb, rows, scale, got_ref, out_ref):
    wg = jnp.zeros((2 * rows, got_ref.shape[2]), jnp.float32)
    for j in range(got_ref.shape[0]):
        wg = wg + got_ref[j, tb:, :].astype(jnp.float32)
    wg = wg * scale
    half = got_ref.shape[2]
    for j in range(out_ref.shape[0]):
        out_ref[j, :, :half] = wg[:rows]
        out_ref[j, :, half:] = wg[rows:]


def weight_part(got, tb, rows, copies, scale):
    width = got.shape[2]
    vmem = pl.BlockSpec(memory_space=pltpu.VMEM)
    return pl.pallas_call(
        functools.partial(weight_part_kernel, tb, rows, scale),
        out_shape=jax.ShapeDtypeStruct((copies, rows, 2 * width), jnp.float32),
        in_specs=[vmem],
        out_specs=vmem,
        cost_estimate=pl.CostEstimate(
            flops=got.shape[0] * 2 * rows * width, transcendentals=0,
            bytes_accessed=got.shape[0] * 2 * rows * width * 2 + copies * rows * 2 * width * 4),
    )(pltpu.with_memory_space_constraint(got, pltpu.VMEM))


def on_device(features, weight, tile_values, tile_rows, tile_cols, tile_count, cotangent):
    rows_dev = features.shape[1]
    width_in = features.shape[2]
    width_out = weight.shape[1]
    tile_size = tile_values.shape[-1]
    n_row = lax.axis_size("row")
    n_col = lax.axis_size("col")
    row_tiles = rows_dev * n_col // tile_size
    col_tiles = rows_dev * n_row // tile_size
    node_total = rows_dev * n_row * n_col
    tile_block = tile_values[0, 0]
    row_ids = tile_rows[0, 0]
    col_ids = tile_cols[0, 0]
    tile_total = tile_count[0, 0]

    gathered = lax.all_to_all(replicate(features, n_row), "row", 0, 0, tiled=False)
    col_source = gathered.reshape(col_tiles, tile_size, width_in)
    partial_value = spread(tile_block, row_ids, col_ids, tile_total, col_source, row_tiles, False, jnp.bfloat16)
    sent = partial_value.reshape(n_col, rows_dev, width_in)
    got = lax.all_to_all(sent, "col", 0, 0, tiled=False)
    out_block, payload = dense(got, weight, cotangent[0])
    output = out_block[None]
    wg_rows = width_in // n_col
    got = lax.all_to_all(payload, "col", 0, 0, tiled=False)
    row_source = got

    payload = spread(
        tile_block, col_ids, row_ids, tile_total, row_source, col_tiles, True, jnp.bfloat16, True
    )
    got = lax.all_to_all(payload, "row", 0, 0, tiled=False)
    grad_features = got[:, :rows_dev].astype(jnp.float32).sum(0).astype(jnp.bfloat16)[None]
    parts = weight_part(got, rows_dev, wg_rows, n_col, node_total ** (-0.5))

    everyone = lax.all_to_all(parts, "col", 0, 0, tiled=False)
    weight_grad = everyone.reshape(width_in, width_out)
    return (output, grad_features, weight_grad)


def solution(mesh):
    placed = (
        P("col", "row", None),
        P(),
        P("row", "col", None, None, None),
        P("row", "col", None),
        P("row", "col", None),
        P("row", "col"),
        P("row", "col", None),
    )
    return jax.shard_map(
        on_device,
        mesh=mesh,
        in_specs=placed,
        out_specs=(P("row", "col", None), P("col", "row", None), P()),
        check_vma=False,
    )
```
